256 devices in a mesh: band: 8 (over z_lo, core), span: 32 (over x, y, z_hi).
Axes of the slice: x: 4, y: 4, z: 8 (z_hi: 2, z_lo: 4; z = z_hi * 4 + z_lo), core: 2. Of those that a mesh axis runs over, the one named last changes fastest.
Arguments:
- gases: bfloat16 [7, 32, 131072], P(None, None, ('band', 'span')), may hold values from 0 to 1
- pressure_bin: int32 [32, 131072], P(None, ('band', 'span')), may hold values from 0 to 59
- layer_mass: bfloat16 [32, 131072], P(None, ('band', 'span')), may hold values from 0.5 to 2
- cos_zenith: bfloat16 [131072], P(('band', 'span')), may hold values from 0.19921875 to 1
- surface_albedo: bfloat16 [131072], P(('band', 'span')), may hold values from 0.049804688 to 0.8984375
- column_order: int32 [131072], P(('band', 'span')), may hold values from 0 to 511, as said below
- sunlit: int32 [1024], P(('band', 'span')), may hold values from 0 to 1, as said below
- absorption: bfloat16 [112, 7, 60], replicated, may hold values from 9.9658966e-05 to 0.099609375
- scattering: bfloat16 [112, 60], replicated, may hold values from 0.19921875 to 0.94921875
Outputs:
- heating: float32 [32, 131072], P(None, ('band', 'span'))
The draws below stay inside these ranges and needn't reach their ends.
Inputs may be any that keep to these rules, and one draw needn't show every extreme that they name: `column_order`: the 512 entries of each device's slice are a permutation of 0 to 511. The 8 devices with the same index along the second mesh axis hold 16 sunlit blocks together; among them one device has all 4 blocks sunlit and one has none.
All inputs are finite; a program needn't handle non-finite values.
Results may differ from the reference program's by a relative error of at most 0.0003.
Values may be sent and summed in bfloat16 or wider, within the bound.
A program may use at most 64 MiB of HBM per device.

```python
import math
import jax
import jax.numpy as jnp
from jax import lax

G = 112
NGAS = 7
K = 60
L = 32
BLK = 128
NB = 4
C_DEV = 512
COLS = 131072
N_BAND = 8
N_SPAN = 32


def draw_column_order(key, part):
    device_count = COLS // C_DEV
    device_keys = jax.random.split(key, device_count)
    orders = jax.vmap(lambda device_key: jax.random.permutation(device_key, C_DEV))(device_keys)
    return orders.reshape(-1).astype(jnp.int32)


def draw_sunlit(key, part):

    def one_group(group_key):
        keys = jax.random.split(group_key, 4)
        counts = jnp.zeros((N_BAND,), jnp.int32).at[0].set(NB)
        if N_BAND > 2:
            values = jax.random.randint(keys[0], ((N_BAND - 2) // 2,), 0, NB + 1).astype(jnp.int32)
            middle = jnp.concatenate([values, NB - values])
            counts = counts.at[1:N_BAND - 1].set(middle)
            unit_moves = jax.random.randint(keys[1], (2 * N_BAND, 2), 1, N_BAND - 1)
            for move_index in range(2 * N_BAND):
                giver_slot = unit_moves[move_index, 0]
                taker_slot = unit_moves[move_index, 1]
                allowed = ((counts[giver_slot] > 0) & (counts[taker_slot] < NB) & (giver_slot != taker_slot)).astype(jnp.int32)
                counts = counts.at[giver_slot].add(-allowed).at[taker_slot].add(allowed)
        placed = jnp.zeros_like(counts).at[jax.random.permutation(keys[2], N_BAND)].set(counts)
        block_keys = jax.random.split(keys[3], N_BAND)
        shuffled = jax.vmap(lambda block_key: jax.random.permutation(block_key, NB))(block_keys)
        return (shuffled < placed[:, None]).astype(jnp.int32)
    group_keys = jax.random.split(key, N_SPAN)
    flags = jax.vmap(one_group)(group_keys)
    return jnp.transpose(flags, (1, 0, 2)).reshape(-1).astype(jnp.int32)


def plant(values, stream_key, smallest, largest):
    extent = values.shape
    place = [jax.random.randint(jax.random.fold_in(stream_key, axis), (), 0, extent[axis]) for axis in range(len(extent))]
    values = values.at[tuple(place)].set(smallest)
    longest = extent.index(max(extent))
    place[longest] = (place[longest] + 1) % extent[longest]
    return values.at[tuple(place)].set(largest)


def level_of(own_key, shape, cuts, smallest, top_value):
    def one(axis_at, shards_of):
        heights = jax.random.uniform(jax.random.fold_in(jax.random.fold_in(own_key, 6), axis_at), (shards_of,), jnp.float32, smallest / len(cuts), top_value / len(cuts))
        return jnp.repeat(jnp.exp(heights), shape[axis_at] // shards_of).reshape((-1,) + (1,) * (len(shape) - axis_at - 1))

    factor_of = one(*cuts[0])
    for cut in cuts[1:]:
        factor_of = factor_of * one(*cut)
    return factor_of


def setup_inputs(seed: int = 0) -> dict:
    key_of = jax.random.split(jax.random.key(seed), 10)
    return {
        "gases": jnp.clip(1.0 * jax.random.uniform(key_of[0], (NGAS, L, COLS), jnp.float32) ** level_of(key_of[0], (NGAS, L, COLS), ((2, 256),), -0.2, 0.2), 0.0, 1.0).astype(jnp.bfloat16),
        "pressure_bin": plant(jax.random.randint(key_of[1], (L, COLS), 0, K), jax.random.fold_in(key_of[1], 1), 0, K - 1).astype(jnp.int32),
        "layer_mass": jnp.clip(jnp.exp(math.log(2.0) - 1.3862944 * jax.random.uniform(key_of[2], (L, COLS), jnp.float32) ** level_of(key_of[2], (L, COLS), ((1, 256),), -0.2, 0.2)), 0.5, 2.0).astype(jnp.bfloat16),
        "cos_zenith": jnp.clip(0.19921875 + 0.80078125 * jax.random.uniform(key_of[3], (COLS,), jnp.float32) ** level_of(key_of[3], (COLS,), ((0, 256),), -0.2, 0.2), 0.19921875, 1.0).astype(jnp.bfloat16),
        "surface_albedo": jnp.clip(0.049804688 + 0.8486328 * jax.random.uniform(key_of[4], (COLS,), jnp.float32) ** level_of(key_of[4], (COLS,), ((0, 256),), -0.2, 0.2), 0.049804688, 0.8984375).astype(jnp.bfloat16),
        "column_order": draw_column_order(jax.random.fold_in(key_of[9], 71), 0),
        "sunlit": draw_sunlit(jax.random.fold_in(key_of[9], 71), 0),
        "absorption": jnp.clip(jnp.exp(jax.random.uniform(key_of[7], (G, NGAS, K), jnp.float32, math.log(9.965896606445312e-05), math.log(0.099609375))), 9.965896606445312e-05, 0.099609375).astype(jnp.bfloat16),
        "scattering": jnp.clip(jax.random.uniform(key_of[8], (G, K), jnp.float32, 0.19921875, 0.94921875), 0.19921875, 0.94921875).astype(jnp.bfloat16),
    }


def column_heating(amounts, bin_index, thickness, cosine, ground, absorption, scattering):
    selector = (bin_index[None] == jnp.arange(K, dtype=jnp.int32)[:, None, None]).astype(jnp.bfloat16)
    weighted = amounts[:, None] * selector[None]
    optical_depth = jnp.einsum("gak,akln->lgn", absorption.astype(jnp.float32), weighted.astype(jnp.float32))
    albedo = jnp.einsum("gk,kln->lgn", scattering.astype(jnp.float32), selector.astype(jnp.float32))
    column_path = jnp.cumsum(optical_depth, axis=0)
    column_path = jnp.concatenate([jnp.zeros_like(column_path[:1]), column_path], axis=0)
    direct = cosine * jnp.exp(-column_path / cosine)
    fading = jnp.exp(-1.66 * optical_depth)
    reflect = 0.5 * albedo * (1.0 - fading)
    transmit = fading + reflect
    source = 0.5 * albedo * (direct[:-1] - direct[1:])

    def upward(state_pair, layer):
        refl_below, source_below = state_pair
        layer_reflect, layer_transmit, layer_source = layer
        denominator = 1.0 - layer_reflect * refl_below
        refl_top = layer_reflect + layer_transmit * layer_transmit * refl_below / denominator
        source_top = layer_source + layer_transmit * (source_below + refl_below * layer_source) / denominator
        return (refl_top, source_top), (refl_top, source_top)

    floor_refl = jnp.broadcast_to(ground, reflect.shape[1:])
    floor_source = ground * direct[-1]
    final_pair, tops = lax.scan(upward, (floor_refl, floor_source), (reflect, transmit, source), reverse=True)
    refl_all = jnp.concatenate([tops[0], floor_refl[None]], axis=0)
    source_all = jnp.concatenate([tops[1], floor_source[None]], axis=0)

    def downward(diffuse, layer):
        layer_reflect, layer_transmit, layer_source, refl_low, source_low = layer
        denominator = 1.0 - layer_reflect * refl_low
        diffuse = (layer_transmit * diffuse + layer_reflect * source_low + layer_source) / denominator
        return diffuse, diffuse

    start_diffuse = jnp.zeros_like(floor_refl)
    final_diffuse, lower = lax.scan(downward, start_diffuse, (reflect, transmit, source, refl_all[1:], source_all[1:]))
    diffuse_all = jnp.concatenate([start_diffuse[None], lower], axis=0)
    net = direct + diffuse_all - (refl_all * diffuse_all + source_all)
    return jnp.sum(net[:-1] - net[1:], axis=1) / thickness


def reference(gases, pressure_bin, layer_mass, cos_zenith, surface_albedo, column_order, sunlit, absorption, scattering):
    device_count = N_BAND * N_SPAN
    per_peer = C_DEV // N_SPAN

    def split(array):
        return jnp.moveaxis(array.reshape(array.shape[:-1] + (device_count, C_DEV)), -2, 0)

    def per_device(inputs):
        amounts, bin_index, thickness, cosine, ground = inputs
        return column_heating(amounts, bin_index, thickness.astype(jnp.float32), cosine.astype(jnp.float32), ground.astype(jnp.float32), absorption, scattering)

    heating = lax.map(per_device, (split(gases), split(pressure_bin), split(layer_mass), split(cos_zenith), split(surface_albedo)))
    block_flag = jnp.repeat(sunlit, BLK).reshape(N_BAND, N_SPAN, N_SPAN, per_peer)
    at_order = jnp.transpose(block_flag, (0, 2, 1, 3)).reshape(device_count, C_DEV)
    ordering = column_order.reshape(device_count, C_DEV)
    dyn_flag = jax.vmap(lambda order_row, flag_row: jnp.zeros((C_DEV,), jnp.int32).at[order_row].set(flag_row))(ordering, at_order)
    heating = heating * dyn_flag[:, None, :].astype(jnp.float32)
    return jnp.moveaxis(heating, 0, 1).reshape(L, device_count * C_DEV)
```

```python
import jax, jax.numpy as jnp
from jax import lax
from jax.experimental import pallas as pl
from jax.experimental.pallas import tpu as pltpu
from jax.sharding import PartitionSpec as P
import functools
MESH = pl.DeviceIdType.MESH
F32=jnp.float32; BF16=jnp.bfloat16
LOG2E=1.4426950408889634

INTERP=False
def rowb(ref,c,row,n):
    if INTERP: return jnp.broadcast_to(ref[c,pl.ds(row,1),:],(n,128))
    return ref[c,pl.ds(row,n,stride=0),:]

def body(gas_ref, bin_ref, mass_ref, cos_ref, alb_ref, order_ref, sun_ref, abs_ref, sca_ref, out_ref,
         gas32, bin32, tab32, lhs, tau_s, h_s, ti_s, v_s, p_s, acc, st32, recv, jcol, loc_sem, ssem, rsem):
    me = lax.axis_index("span")
    q = me // 2
    zh = lax.rem(me, 2)
    def peer(d): return {"span": lax.rem(q + d, 16) * 2 + zh}
    def row(d): return zh * 16 + lax.rem(q + d, 16)
    across = {"span": q * 2 + 1 - zh}
    barrier = pltpu.get_barrier_semaphore()
    for d in range(1, 16):
        pl.semaphore_signal(barrier, inc=1, device_id=peer(d), device_id_type=MESH)
    pl.semaphore_signal(barrier, inc=1, device_id=across, device_id_type=MESH)
    own = pltpu.make_async_copy(sun_ref, recv.at[row(0)], loc_sem)
    own.start()
    def flat(d, r):
        return pltpu.make_async_remote_copy(src_ref=sun_ref, dst_ref=recv.at[r], send_sem=ssem.at[d], recv_sem=rsem.at[d],
            device_id=peer(d), device_id_type=MESH)
    def deep(z):
        return pltpu.make_async_remote_copy(src_ref=recv.at[pl.ds(zh * 16, 16)], dst_ref=recv.at[pl.ds(z * 16, 16)],
            send_sem=ssem.at[0], recv_sem=rsem.at[0], device_id=across, device_id_type=MESH)
    trow = lax.broadcasted_iota(jnp.int32, (8, 512), 1)
    trow = (lax.rem(trow // 16, 2) * 16 + trow // 32).astype(F32).astype(BF16)
    order = order_ref[...].reshape(1, 512)
    for c in range(4):
        hot = (lax.broadcasted_iota(jnp.int32, (128, 512), 0) + c * 128 == order).astype(F32).astype(BF16)
        jcol[:, c*128:c*128+128] = lax.dot_general(trow, hot, (((1,), (1,)), ((), ())), preferred_element_type=F32)
    for c in range(4):
        gas32[c] = gas_ref[:,:,c*128:c*128+128].reshape(7*32,128).astype(F32)
        bin32[c] = bin_ref[:,c*128:c*128+128].astype(F32)
    tab32[...] = jnp.zeros_like(tab32)
    for a in range(7):
        tab32[a*64:a*64+60, :112] = abs_ref[a].astype(F32)
    tab32[448:508, :112] = sca_ref[...].astype(F32)*0.5
    lhs[...] = jnp.transpose(tab32[...])[:112].astype(BF16)
    kk = lax.broadcasted_iota(jnp.int32,(64,256),0).astype(F32).astype(BF16)

    @pl.loop(0,32)
    def _(l):
        for g in range(2):
            cs = pl.ds(g*256,256)
            def bc(ref,row):
                return jnp.concatenate([rowb(ref,2*g+q,row,16) for q in range(2)],axis=1).astype(BF16)
            kb = bc(bin32,l)
            kb = jnp.concatenate([kb]*4,axis=0)
            m = (kb==kk)
            ws=[]
            for a in range(7):
                ab = bc(gas32,a*32+l)
                ab = jnp.concatenate([ab]*4,axis=0)
                ws.append(jnp.where(m,ab,jnp.zeros_like(ab)))
            sel = jnp.where(m,jnp.ones_like(ab),jnp.zeros_like(ab))
            W = jnp.concatenate(ws,axis=0)
            tau_s[l,:,cs] = jnp.dot(lhs[:, :448], W, preferred_element_type=F32)
            h_s[l,:,cs] = jnp.dot(lhs[:, 448:], sel, preferred_element_type=F32)

    pl.semaphore_wait(barrier, 16)
    for d in range(1, 16):
        flat(d, row(0)).start()

    mu = cos_ref[...].astype(F32).reshape(1,512)
    al = alb_ref[...].astype(F32).reshape(1,512)
    mb=-LOG2E/mu
    for c in range(4):
        st32[c,0:1,:]=mb[:,c*128:c*128+128]
        st32[c,1:2,:]=al[:,c*128:c*128+128]
    acc[...] = jnp.zeros_like(acc)
    NT=7
    for c in range(4):
        if c == 2:
            own.wait()
            for d in range(1, 16):
                flat(d, row(0)).wait_send()
                flat(d, row(16 - d)).wait_recv()
            deep(zh).start()
        cs = pl.ds(c*128,128)
        cmu = rowb(st32,c,0,8)
        alb = rowb(st32,c,1,8)
        for hf in range(2):
            def gs(i): return pl.ds((hf*NT+i)*8,8)
            zero = jnp.zeros((8,128),F32); one=jnp.ones((8,128),F32)
            def down(l,carry):
                cum,T,Pp,Q = carry
                ncum=[];nT=[];nP=[];nQ=[]
                x = None
                for i in range(NT):
                    tau = tau_s[l,gs(i),cs]; h = h_s[l,gs(i),cs]
                    c1 = cum[i]+tau
                    T1 = jnp.exp2(c1*cmu)
                    f = jnp.exp2(tau*(-1.66*LOG2E))
                    r = h*(1.0-f)
                    t = f+r
                    s = h*(T[i]-T1)
                    den = 1.0-r*Pp[i]
                    y = pl.reciprocal(den,approx=True)
                    inv = y*(2.0-den*y)
                    ti = t*inv
                    v = (r*Q[i]+s)*inv
                    a = ti*Pp[i]
                    b = Pp[i]*v+Q[i]
                    ti_s[l,gs(i),cs]=ti
                    v_s[l,gs(i),cs]=v
                    p_s[l,gs(i),cs]=a-ti
                    xx = T[i]+(b-v)
                    x = xx if x is None else x+xx
                    ncum.append(c1);nT.append(T1);nP.append(r+t*a);nQ.append(s+t*b)
                acc[l,:,cs] = acc[l,:,cs]+x
                return (tuple(ncum),tuple(nT),tuple(nP),tuple(nQ))
            z=(zero,)*NT
            cum,T,Pp,Q = lax.fori_loop(0,32,down,(z,(one,)*NT,z,z))
            U=[]; x=None
            for i in range(NT):
                u = alb*(Q[i]+T[i])/(1.0-alb*Pp[i])
                d = Pp[i]*u+Q[i]
                xx = T[i]+d-u
                x = xx if x is None else x+xx
                U.append(u)
            acc[32,:,cs] = acc[32,:,cs]+x
            def up(k,U):
                l = 31-k
                x=None; nU=[]
                for i in range(NT):
                    xx = p_s[l,gs(i),cs]*U[i]
                    nU.append(ti_s[l,gs(i),cs]*U[i]+v_s[l,gs(i),cs])
                    x = xx if x is None else x+xx
                acc[l,:,cs] = acc[l,:,cs]+x
                return tuple(nU)
            lax.fori_loop(0,32,up,tuple(U))
    deep(zh).wait_send()
    deep(1 - zh).wait_recv()
    flags = recv[...].reshape(32, 4)
    mine = lax.broadcasted_iota(jnp.int32, (32, 4), 1) == me // 8
    flag = jnp.sum(jnp.where(mine, flags, 0).astype(F32), axis=1, keepdims=True)
    j = lax.broadcasted_iota(jnp.int32, (32, 512), 0).astype(F32)
    lit = jnp.sum(jnp.where(jnp.broadcast_to(jcol[0:1, :], (32, 512)) == j, jnp.broadcast_to(flag, (32, 512)), 0.0), axis=0, keepdims=True)
    tot = jnp.sum(acc[...],axis=1)
    out_ref[...] = (tot[:32]-tot[1:])*(lit*mu/mass_ref[...].astype(F32))

def call(*args):
    args=list(args); args[7]=jnp.transpose(args[7],(1,2,0)); args[8]=jnp.transpose(args[8]); args[6]=args[6].reshape(1,4)
    vm = pl.BlockSpec(memory_space=pltpu.VMEM)
    return pl.pallas_call(body, out_shape=jax.ShapeDtypeStruct((32,512),F32),
        in_specs=[vm]*9, out_specs=vm,
        scratch_shapes=[pltpu.VMEM((4,224,128),F32),pltpu.VMEM((4,32,128),F32),pltpu.VMEM((512,128),F32),pltpu.VMEM((112,512),BF16)]
          +[pltpu.VMEM((32,112,512),F32)]*5+[pltpu.VMEM((33,8,512),F32),pltpu.VMEM((4,8,128),F32),
          pltpu.VMEM((32,1,4),jnp.int32),pltpu.VMEM((8,512),F32),pltpu.SemaphoreType.DMA,pltpu.SemaphoreType.DMA((16,)),pltpu.SemaphoreType.DMA((16,))],
        compiler_params=pltpu.CompilerParams(vmem_limit_bytes=60*1024*1024, collective_id=0, has_side_effects=True),
        )(*args)

def solution(mesh):
    s1=P(("band","span"))
    placed=(P(None,None,("band","span")),P(None,("band","span")),P(None,("band","span")),s1,s1,s1,s1,P(),P())
    return jax.shard_map(call,mesh=mesh,in_specs=placed,out_specs=P(None,("band","span")),check_vma=False)
```

```python
import jax
import jax.numpy as jnp
from jax import lax
from jax.experimental import pallas as pl
from jax.experimental.pallas import tpu as pltpu
from jax.sharding import PartitionSpec as P

MESH = pl.DeviceIdType.MESH
F32 = jnp.float32
BF16 = jnp.bfloat16
LOG2E = 1.4426950408889634
FADE = -1.66 * LOG2E
LANES = 128
GAS = 7
L = 32
G = 112
C = 512
TILES = G // 8
INTERP = False


def wide_row(ref, c, row, n):
    if INTERP:
        return jnp.broadcast_to(ref[c, pl.ds(row, 1), :], (n, LANES))
    return ref[c, pl.ds(row, n, stride=0), :]


def cols(c):
    return slice(c * LANES, (c + 1) * LANES)


def rows(i):
    return slice(i * 8, (i + 1) * 8)


def body(gas_hbm, bin_hbm, mass_hbm, cos_hbm, alb_hbm, order_hbm, sun_ref, abs_hbm, sca_hbm, out_ref,
         gas_ref, bin_ref, mass_ref, cos_ref, alb_ref, order_ref, abs_ref, sca_ref,
         gas32, bin32, tab32, lhs, tau_a, tau_b, h_a, h_b, st_t, st_p, st_q, ti_s, v_s, p_s, acc, per_col,
         heat, recv, jcol, loc_sem, ssem, rsem):
    me = lax.axis_index("span")
    x = me // 8
    y = lax.rem(me // 2, 4)
    zh = lax.rem(me, 2)
    zl = lax.axis_index("band") // 2
    hops = jnp.minimum(x, 2) + jnp.minimum(y, 2)
    moment = jnp.where(zh == 0, (36 - 5 * hops) // 2, jnp.maximum((11 + 3 * zl - 3 * hops) // 2, 0))
    barrier = pltpu.get_barrier_semaphore()

    def turn(d):
        return lax.rem(me + d, 32)

    for d in range(1, 32):
        pl.semaphore_signal(barrier, inc=1, device_id={"span": turn(d)}, device_id_type=MESH)

    loads = [pltpu.make_async_copy(src, dst, loc_sem.at[n]) for n, (src, dst) in enumerate((
        (abs_hbm, abs_ref), (sca_hbm, sca_ref), (gas_hbm, gas_ref), (bin_hbm, bin_ref), (cos_hbm, cos_ref),
        (alb_hbm, alb_ref), (order_hbm, order_ref), (mass_hbm, mass_ref), (sun_ref, recv.at[me])))]
    for v in loads:
        v.start()

    def flag_copy(r, d):
        return pltpu.make_async_remote_copy(
            src_ref=sun_ref, dst_ref=recv.at[r], send_sem=ssem.at[d], recv_sem=rsem.at[d],
            device_id={"span": turn(d)}, device_id_type=MESH)

    def send(when):
        @pl.when(when)
        def _():
            pl.semaphore_wait(barrier, 31)
            for d in range(1, 32):
                flag_copy(me, d).start()

    send(moment == 0)
    for v in loads:
        v.wait()

    for c in range(4):
        gas32[c] = gas_ref[:, :, cols(c)].reshape(GAS * L, LANES).astype(F32)
        bin32[c] = bin_ref[:, cols(c)].astype(F32)
    tab32[...] = jnp.zeros_like(tab32)
    for a in range(GAS):
        tab32[a * 64:a * 64 + 60, :G] = abs_ref[a].astype(F32)
    tab32[448:508, :G] = sca_ref[...].astype(F32) * 0.5
    lhs[...] = jnp.transpose(tab32[...])[:G].astype(BF16)
    kk = lax.broadcasted_iota(jnp.int32, (64, 256), 0).astype(F32).astype(BF16)

    def optics(l, tau_ref, h_ref):
        for g in range(2):
            def spread(ref, r):
                x = jnp.concatenate([wide_row(ref, 2 * g + k, r, 16) for k in range(2)], axis=1).astype(BF16)
                return jnp.concatenate([x] * 4, axis=0)

            here = spread(bin32, l) == kk
            zero = jnp.zeros((64, 256), BF16)
            w = jnp.concatenate([jnp.where(here, spread(gas32, a * L + l), zero) for a in range(GAS)], axis=0)
            sel = jnp.where(here, jnp.ones_like(zero), zero)
            cs = slice(g * 256, g * 256 + 256)
            tau_ref[:, cs] = jnp.dot(lhs[:, :448], w, preferred_element_type=F32)
            h_ref[:, cs] = jnp.dot(lhs[:, 448:], sel, preferred_element_type=F32)

    optics(0, tau_a, h_a)
    mu = cos_ref[...].astype(F32).reshape(1, C)
    rate = -LOG2E / mu
    alb = alb_ref[...].astype(F32).reshape(1, C)
    for c in range(4):
        per_col[c, 0:1, :] = rate[:, cols(c)]
        per_col[c, 1:2, :] = alb[:, cols(c)]
    st_t[...] = jnp.ones_like(st_t)
    st_p[...] = jnp.zeros_like(st_p)
    st_q[...] = jnp.zeros_like(st_q)

    def layer(l, tau_ref, h_ref):
        for c in range(4):
            cs = cols(c)
            rate = wide_row(per_col, c, 0, 8)
            x = None
            for i in range(TILES):
                gs = rows(i)
                tau = tau_ref[gs, cs]
                h = h_ref[gs, cs]
                t0 = st_t[gs, cs]
                p0 = st_p[gs, cs]
                q0 = st_q[gs, cs]
                t1 = t0 * jnp.exp2(tau * rate)
                f = jnp.exp2(tau * FADE)
                r = h * (1.0 - f)
                t = f + r
                s = h * (t0 - t1)
                inv = pl.reciprocal(1.0 - r * p0, approx=False)
                ti = t * inv
                y = q0 + p0 * s
                st_t[gs, cs] = t1
                st_p[gs, cs] = r + t * (ti * p0)
                st_q[gs, cs] = s + ti * y
                ti_s[l, gs, cs] = ti
                v_s[l, gs, cs] = inv * (r * q0 + s)
                p_s[l, gs, cs] = p0
                x = t0 + q0 if x is None else x + (t0 + q0)
            acc[l, :, cs] = x

    def pair(k, carry):
        l = 2 * k
        send((k > 0) & (k == moment))
        optics(l + 1, tau_b, h_b)
        layer(l, tau_a, h_a)
        optics(jnp.minimum(l + 2, L - 1), tau_a, h_a)
        layer(l + 1, tau_b, h_b)
        return carry

    lax.fori_loop(0, L // 2, pair, 0)

    trow = lax.broadcasted_iota(jnp.int32, (8, C), 1)
    trow = (trow // 16).astype(F32).astype(BF16)
    order = order_ref[...].reshape(1, C)
    for c in range(4):
        hot = (lax.broadcasted_iota(jnp.int32, (LANES, C), 0) + c * LANES == order).astype(F32).astype(BF16)
        jcol[:, cols(c)] = lax.dot_general(trow, hot, (((1,), (1,)), ((), ())), preferred_element_type=F32)

    for half in range(2):
        where = [(rows(i), cols(c)) for c in (2 * half, 2 * half + 1) for i in range(TILES)]
        up0 = []
        sums = []
        for n, (gs, cs) in enumerate(where):
            al = wide_row(per_col, 2 * half + n // TILES, 1, 8)
            tt = st_t[gs, cs]
            pp = st_p[gs, cs]
            qq = st_q[gs, cs]
            u = al * (qq + tt) / (1.0 - al * pp)
            up0.append(u)
            sums.append(tt + (pp * u + qq) - u)
        for j in range(2):
            acc[L, :, cols(2 * half + j)] = sum(sums[j * TILES + 1:(j + 1) * TILES], sums[j * TILES])

        def up(k, u):
            for l in (L - 1 - 2 * k, L - 2 - 2 * k):
                u = [ti_s[l, gs, cs] * u[n] + v_s[l, gs, cs] for n, (gs, cs) in enumerate(where)]
                d = [p_s[l, gs, cs] * u[n] - u[n] for n, (gs, cs) in enumerate(where)]
                for j in range(2):
                    cs = cols(2 * half + j)
                    acc[l, :, cs] = acc[l, :, cs] + sum(d[j * TILES + 1:(j + 1) * TILES], d[j * TILES])
            return tuple(u)

        lax.fori_loop(0, L // 2, up, tuple(up0))
        if half == 0:
            send(moment >= L // 2)

    net = jnp.sum(acc[...], axis=1)
    heat[...] = (net[:L] - net[1:]) * (mu / mass_ref[...].astype(F32))
    for d in range(1, 32):
        flag_copy(turn(32 - d), d).wait_recv()
    flags = recv[...].reshape(32, 4)
    mine = lax.broadcasted_iota(jnp.int32, (32, 4), 1) == me // 8
    flag = jnp.sum(jnp.where(mine, flags, 0).astype(F32), axis=1, keepdims=True)
    j = lax.broadcasted_iota(jnp.int32, (32, C), 0).astype(F32)
    lit = jnp.sum(jnp.where(jnp.broadcast_to(jcol[0:1, :], (32, C)) == j, jnp.broadcast_to(flag, (32, C)), 0.0),
                  axis=0, keepdims=True)
    out_ref[...] = heat[...] * lit

    for d in range(1, 32):
        flag_copy(me, d).wait_send()


def local(gases, pressure_bin, layer_mass, cos_zenith, surface_albedo, column_order, sunlit, absorption, scattering):
    vm = pl.BlockSpec(memory_space=pltpu.VMEM)
    state = [pltpu.VMEM((G, C), F32)]
    return pl.pallas_call(
        body,
        out_shape=pltpu.VMEM((L, C), F32),
        in_specs=[pl.BlockSpec(memory_space=pl.ANY)] * 9,
        out_specs=vm,
        scratch_shapes=[
            pltpu.VMEM((GAS, L, C), BF16), pltpu.VMEM((L, C), jnp.int32), pltpu.VMEM((L, C), BF16),
            pltpu.VMEM((C,), BF16), pltpu.VMEM((C,), BF16), pltpu.VMEM((C,), jnp.int32),
            pltpu.VMEM((GAS, 60, G), BF16), pltpu.VMEM((60, G), BF16),
            pltpu.VMEM((4, GAS * L, LANES), F32), pltpu.VMEM((4, L, LANES), F32), pltpu.VMEM((C, LANES), F32),
            pltpu.VMEM((G, C), BF16)] + state * 7 + [pltpu.VMEM((L, G, C), F32)] * 3 + [
            pltpu.VMEM((L + 1, 8, C), F32), pltpu.VMEM((4, 8, LANES), F32),
            pltpu.VMEM((L, C), F32), pltpu.VMEM((32, 1, 4), jnp.int32), pltpu.VMEM((8, C), F32),
            pltpu.SemaphoreType.DMA((9,)), pltpu.SemaphoreType.DMA((32,)), pltpu.SemaphoreType.DMA((32,))],
        compiler_params=pltpu.CompilerParams(
            vmem_limit_bytes=60 * 1024 * 1024, collective_id=0, has_side_effects=True),
    )(gases, pressure_bin, layer_mass, cos_zenith, surface_albedo, column_order, sunlit.reshape(1, 4),
      jnp.transpose(absorption, (1, 2, 0)), jnp.transpose(scattering))


def solution(mesh):
    one = P(("band", "span"))
    two = P(None, ("band", "span"))
    return jax.shard_map(
        local, mesh=mesh, in_specs=(P(None, None, ("band", "span")), two, two, one, one, one, one, P(), P()),
        out_specs=two, check_vma=False)
```

```python
import jax
import jax.numpy as jnp
from jax import lax
from jax.experimental import pallas as pl
from jax.experimental.pallas import tpu as pltpu
from jax.sharding import PartitionSpec as P

MESH = pl.DeviceIdType.MESH
F32 = jnp.float32
BF16 = jnp.bfloat16
LOG2E = 1.4426950408889634
FADE = -1.66 * LOG2E
LANES = 128
GAS = 7
L = 32
G = 112
C = 512
TILES = G // 8
INTERP = False


def wide_row(ref, c, row, n):
    if INTERP:
        return jnp.broadcast_to(ref[c, pl.ds(row, 1), :], (n, LANES))
    return ref[c, pl.ds(row, n, stride=0), :]


def cols(c):
    return slice(c * LANES, (c + 1) * LANES)


def rows(i):
    return slice(i * 8, (i + 1) * 8)


def body(gas_hbm, bin_hbm, mass_hbm, cos_hbm, alb_hbm, order_hbm, sun_ref, abs_hbm, sca_hbm, out_ref,
         gas_ref, bin_ref, mass_ref, cos_ref, alb_ref, order_ref, abs_ref, sca_ref,
         gas32, bin32, tab32, lhs, tau_a, tau_b, h_a, h_b, st_t, st_p, st_q, ti_s, v_s, p_s, acc, per_col,
         heat, recv, jcol, loc_sem, ssem, rsem):
    me = lax.axis_index("span")
    q = me // 2
    zh = lax.rem(me, 2)
    x = q // 4
    y = lax.rem(q, 4)
    zl = lax.axis_index("band") // 2
    hops = jnp.minimum(x, 2) + jnp.minimum(y, 2)
    direct = zl >= 2
    first = zh == 0
    own_row = first | direct
    mine = zh * 16 + q
    moment = jnp.where(direct, jnp.where(first, 35 - 3 * zl - 3 * hops, 9 + 3 * zl - 3 * hops),
                       jnp.where(first, 24 - 3 * hops, jnp.maximum(6 + 3 * zl - 3 * hops, 0))) // 2
    expected = jnp.where(direct, 31, jnp.where(first, 15, 16))
    barrier = pltpu.get_barrier_semaphore()

    def turn(d):
        return lax.rem(q + d, 16)

    def device(plane, d):
        return {"span": turn(d) * 2 + plane}

    def each(plane, act):
        for d in range(16):
            if d:
                act(plane, d)
            else:
                pl.when(zh != plane)(lambda: act(plane, 0))

    def signal(plane, d):
        pl.semaphore_signal(barrier, inc=1, device_id=device(plane, d), device_id_type=MESH)

    @pl.when(own_row)
    def _():
        each(1, signal)
        each(0, signal)

    loads = [pltpu.make_async_copy(src, dst, loc_sem.at[n]) for n, (src, dst) in enumerate((
        (abs_hbm, abs_ref), (sca_hbm, sca_ref), (gas_hbm, gas_ref), (bin_hbm, bin_ref), (cos_hbm, cos_ref),
        (alb_hbm, alb_ref), (order_hbm, order_ref), (mass_hbm, mass_ref)))]
    own = pltpu.make_async_copy(sun_ref, recv.at[mine], loc_sem.at[8])
    for v in loads:
        v.start()
    pl.when(own_row)(lambda: own.start())

    def flag_copy(r, plane, d):
        return pltpu.make_async_remote_copy(
            src_ref=sun_ref, dst_ref=recv.at[r], send_sem=ssem.at[plane * 16 + d], recv_sem=rsem.at[r],
            device_id=device(plane, d), device_id_type=MESH)

    def table_copy():
        return pltpu.make_async_remote_copy(
            src_ref=recv, dst_ref=recv, send_sem=ssem.at[32], recv_sem=rsem.at[32],
            device_id={"span": q * 2 + 1 - zh}, device_id_type=MESH)

    def start_copy(plane, d):
        flag_copy(mine, plane, d).start()

    def end_copy(plane, d):
        flag_copy(mine, plane, d).wait_send()

    def take_row(plane, d):
        flag_copy(plane * 16 + turn(d), plane, d).wait_recv()

    def send(when):
        @pl.when(when)
        def _():
            pl.semaphore_wait(barrier, expected)
            each(0, start_copy)
            pl.when(direct)(lambda: each(1, start_copy))

    def take_rows(when):
        @pl.when(when)
        def _():
            own.wait()
            each(0, take_row)
            each(1, take_row)

    def hand_over():
        take_rows(first & jnp.logical_not(direct))
        pl.when(first & jnp.logical_not(direct))(lambda: table_copy().start())

    def finish_rows():
        take_rows(direct)
        pl.when(jnp.logical_not(own_row))(lambda: table_copy().wait_recv())

    def end_copies():
        each(0, end_copy)
        pl.when(direct)(lambda: each(1, end_copy))
        pl.when(first & jnp.logical_not(direct))(lambda: table_copy().wait_send())

    send(moment == 0)
    for v in loads:
        v.wait()

    for c in range(4):
        gas32[c] = gas_ref[:, :, cols(c)].reshape(GAS * L, LANES).astype(F32)
        bin32[c] = bin_ref[:, cols(c)].astype(F32)
    tab32[...] = jnp.zeros_like(tab32)
    for a in range(GAS):
        tab32[a * 64:a * 64 + 60, :G] = abs_ref[a].astype(F32)
    tab32[448:508, :G] = sca_ref[...].astype(F32) * 0.5
    lhs[...] = jnp.transpose(tab32[...])[:G].astype(BF16)
    kk = lax.broadcasted_iota(jnp.int32, (64, 256), 0).astype(F32).astype(BF16)

    def optics(l, tau_ref, h_ref, groups=(0, 1), after=None):
        for g in groups:
            def spread(ref, r):
                x = jnp.concatenate([wide_row(ref, 2 * g + k, r, 16) for k in range(2)], axis=1)
                if ref is bin32 and after is not None:
                    z = jnp.concatenate([after * 0.0] * 2, axis=0)
                    x = x + jnp.concatenate([z, z], axis=1)
                x = x.astype(BF16)
                return jnp.concatenate([x] * 4, axis=0)

            here = spread(bin32, l) == kk
            zero = jnp.zeros((64, 256), BF16)
            w = jnp.concatenate([jnp.where(here, spread(gas32, a * L + l), zero) for a in range(GAS)], axis=0)
            sel = jnp.where(here, jnp.ones_like(zero), zero)
            cs = slice(g * 256, g * 256 + 256)
            tau_ref[:, cs] = jnp.dot(lhs[:, :448], w, preferred_element_type=F32)
            h_ref[:, cs] = jnp.dot(lhs[:, 448:], sel, preferred_element_type=F32)

    optics(0, tau_a, h_a)
    mu = cos_ref[...].astype(F32).reshape(1, C)
    rate = -LOG2E / mu
    alb = alb_ref[...].astype(F32).reshape(1, C)
    for c in range(4):
        per_col[c, 0:1, :] = rate[:, cols(c)]
        per_col[c, 1:2, :] = alb[:, cols(c)]
    st_t[...] = jnp.ones_like(st_t)
    st_p[...] = jnp.zeros_like(st_p)
    st_q[...] = jnp.zeros_like(st_q)

    def layer(l, tau_ref, h_ref, tiles):
        seen = []
        for c in tiles:
            cs = cols(c)
            rate = wide_row(per_col, c, 0, 8)
            x = None
            for i in range(TILES):
                gs = rows(i)
                tau = tau_ref[gs, cs]
                h = h_ref[gs, cs]
                t0 = st_t[gs, cs]
                p0 = st_p[gs, cs]
                q0 = st_q[gs, cs]
                t1 = t0 * jnp.exp2(tau * rate)
                f = jnp.exp2(tau * FADE)
                r = h * (1.0 - f)
                t = f + r
                s = h * (t0 - t1)
                inv = pl.reciprocal(1.0 - r * p0, approx=False)
                ti = t * inv
                y = q0 + p0 * s
                st_t[gs, cs] = t1
                st_p[gs, cs] = r + t * (ti * p0)
                st_q[gs, cs] = s + ti * y
                ti_s[l, gs, cs] = ti
                v_s[l, gs, cs] = inv * (r * q0 + s)
                p_s[l, gs, cs] = p0
                x = t0 + q0 if x is None else x + (t0 + q0)
            acc[l, :, cs] = x
            seen.append(x)
        return seen

    def pair(k, carry):
        l = 2 * k
        send((k > 0) & (k == moment))
        n = jnp.minimum(l + 2, L - 1)
        x = layer(l, tau_a, h_a, (0, 1))
        optics(l + 1, tau_b, h_b, (0,))
        optics(l + 1, tau_b, h_b, (1,), x[0])
        y = layer(l, tau_a, h_a, (2, 3))
        x = layer(l + 1, tau_b, h_b, (0, 1))
        optics(n, tau_a, h_a, (0,), y[1])
        optics(n, tau_a, h_a, (1,), x[0])
        layer(l + 1, tau_b, h_b, (2, 3))
        return carry

    lax.fori_loop(0, L // 2, pair, 0)

    trow = lax.broadcasted_iota(jnp.int32, (8, C), 1)
    trow = (lax.rem(trow // 16, 2) * 16 + trow // 32).astype(F32).astype(BF16)
    order = order_ref[...].reshape(1, C)
    for c in range(4):
        hot = (lax.broadcasted_iota(jnp.int32, (LANES, C), 0) + c * LANES == order).astype(F32).astype(BF16)
        jcol[:, cols(c)] = lax.dot_general(trow, hot, (((1,), (1,)), ((), ())), preferred_element_type=F32)

    for half in range(2):
        where = [(rows(i), cols(c)) for c in (2 * half, 2 * half + 1) for i in range(TILES)]
        up0 = []
        sums = []
        for n, (gs, cs) in enumerate(where):
            al = wide_row(per_col, 2 * half + n // TILES, 1, 8)
            tt = st_t[gs, cs]
            pp = st_p[gs, cs]
            qq = st_q[gs, cs]
            u = al * (qq + tt) / (1.0 - al * pp)
            up0.append(u)
            sums.append(tt + (pp * u + qq) - u)
        for j in range(2):
            acc[L, :, cols(2 * half + j)] = sum(sums[j * TILES + 1:(j + 1) * TILES], sums[j * TILES])

        def up(k, u):
            for l in (L - 1 - 2 * k, L - 2 - 2 * k):
                u = [ti_s[l, gs, cs] * u[n] + v_s[l, gs, cs] for n, (gs, cs) in enumerate(where)]
                d = [p_s[l, gs, cs] * u[n] - u[n] for n, (gs, cs) in enumerate(where)]
                for j in range(2):
                    cs = cols(2 * half + j)
                    acc[l, :, cs] = acc[l, :, cs] + sum(d[j * TILES + 1:(j + 1) * TILES], d[j * TILES])
            return tuple(u)

        lax.fori_loop(0, L // 2, up, tuple(up0))

    hand_over()
    net = jnp.sum(acc[...], axis=1)
    heat[...] = (net[:L] - net[1:]) * (mu / mass_ref[...].astype(F32))
    finish_rows()
    flags = recv[...].reshape(32, 4)
    block = lax.broadcasted_iota(jnp.int32, (32, 4), 1) == me // 8
    flag = jnp.sum(jnp.where(block, flags, 0).astype(F32), axis=1, keepdims=True)
    j = lax.broadcasted_iota(jnp.int32, (32, C), 0).astype(F32)
    lit = jnp.sum(jnp.where(jnp.broadcast_to(jcol[0:1, :], (32, C)) == j, jnp.broadcast_to(flag, (32, C)), 0.0),
                  axis=0, keepdims=True)
    out_ref[...] = heat[...] * lit

    end_copies()


def local(gases, pressure_bin, layer_mass, cos_zenith, surface_albedo, column_order, sunlit, absorption, scattering):
    vm = pl.BlockSpec(memory_space=pltpu.VMEM)
    state = [pltpu.VMEM((G, C), F32)]
    return pl.pallas_call(
        body,
        out_shape=pltpu.VMEM((L, C), F32),
        in_specs=[pl.BlockSpec(memory_space=pl.ANY)] * 9,
        out_specs=vm,
        scratch_shapes=[
            pltpu.VMEM((GAS, L, C), BF16), pltpu.VMEM((L, C), jnp.int32), pltpu.VMEM((L, C), BF16),
            pltpu.VMEM((C,), BF16), pltpu.VMEM((C,), BF16), pltpu.VMEM((C,), jnp.int32),
            pltpu.VMEM((GAS, 60, G), BF16), pltpu.VMEM((60, G), BF16),
            pltpu.VMEM((4, GAS * L, LANES), F32), pltpu.VMEM((4, L, LANES), F32), pltpu.VMEM((C, LANES), F32),
            pltpu.VMEM((G, C), BF16)] + state * 7 + [pltpu.VMEM((L, G, C), F32)] * 3 + [
            pltpu.VMEM((L + 1, 8, C), F32), pltpu.VMEM((4, 8, LANES), F32),
            pltpu.VMEM((L, C), F32), pltpu.VMEM((32, 1, 4), jnp.int32), pltpu.VMEM((8, C), F32),
            pltpu.SemaphoreType.DMA((9,)), pltpu.SemaphoreType.DMA((33,)), pltpu.SemaphoreType.DMA((33,))],
        compiler_params=pltpu.CompilerParams(
            vmem_limit_bytes=60 * 1024 * 1024, collective_id=0, has_side_effects=True),
    )(gases, pressure_bin, layer_mass, cos_zenith, surface_albedo, column_order, sunlit.reshape(1, 4),
      jnp.transpose(absorption, (1, 2, 0)), jnp.transpose(scattering))


def solution(mesh):
    one = P(("band", "span"))
    two = P(None, ("band", "span"))
    return jax.shard_map(
        local, mesh=mesh, in_specs=(P(None, None, ("band", "span")), two, two, one, one, one, one, P(), P()),
        out_specs=two, check_vma=False)
```

```python
import jax
import jax.numpy as jnp
from jax import lax
from jax.experimental import pallas as pl
from jax.experimental.pallas import tpu as pltpu
from jax.sharding import PartitionSpec as P

MESH = pl.DeviceIdType.MESH
F32 = jnp.float32
BF16 = jnp.bfloat16
LOG2E = 1.4426950408889634
FADE = -1.66 * LOG2E
LANES = 128
GAS = 7
L = 32
G = 112
C = 512
TILES = G // 8
INTERP = False


def wide_row(ref, c, row, n):
    if INTERP:
        return jnp.broadcast_to(ref[c, pl.ds(row, 1), :], (n, LANES))
    return ref[c, pl.ds(row, n, stride=0), :]


def cols(c):
    return slice(c * LANES, (c + 1) * LANES)


def rows(i):
    return slice(i * 8, (i + 1) * 8)


def body(gas_hbm, bin_hbm, mass_hbm, cos_hbm, alb_hbm, order_hbm, sun_ref, abs_hbm, sca_hbm, out_ref,
         gas_ref, bin_ref, mass_ref, cos_ref, alb_ref, order_ref, abs_ref, sca_ref,
         gas32, bin32, tab32, lhs, tau_a, tau_b, h_a, h_b, st_t, st_p, st_q, ti_s, v_s, p_s, acc, per_col,
         heat, recv, jcol, loc_sem, ssem, rsem):
    me = lax.axis_index("span")
    q = me // 2
    zh = lax.rem(me, 2)
    x = q // 4
    y = lax.rem(q, 4)
    zl = lax.axis_index("band") // 2
    hops = jnp.minimum(x, 2) + jnp.minimum(y, 2)
    direct = zl >= 2
    first = zh == 0
    corner = (zh == 1) & (q == 0) & jnp.logical_not(direct)
    own_row = first | direct | corner
    to_corner = jnp.logical_not(direct | corner)
    mine = zh * 16 + q
    moment = jnp.where(direct, jnp.where(first, 35 - 3 * zl - 3 * hops, 9 + 3 * zl - 3 * hops),
                       jnp.where(first, 24 - 5 * hops // 2, jnp.maximum(6 + 3 * zl - 3 * hops, 0))) // 2
    expected = jnp.where(direct, 31, jnp.where(first | corner, 16, 17))
    barrier = pltpu.get_barrier_semaphore()

    def turn(d):
        return lax.rem(q + d, 16)

    def device(plane, d):
        return {"span": turn(d) * 2 + plane}

    def each(plane, act):
        for d in range(16):
            if d:
                act(plane, d)
            else:
                pl.when(zh != plane)(lambda: act(plane, 0))

    def signal(plane, d):
        pl.semaphore_signal(barrier, inc=1, device_id=device(plane, d), device_id_type=MESH)

    @pl.when(own_row)
    def _():
        each(1, signal)
        each(0, signal)

    loads = [pltpu.make_async_copy(src, dst, loc_sem.at[n]) for n, (src, dst) in enumerate((
        (abs_hbm, abs_ref), (sca_hbm, sca_ref), (gas_hbm, gas_ref), (bin_hbm, bin_ref), (cos_hbm, cos_ref),
        (alb_hbm, alb_ref), (order_hbm, order_ref), (mass_hbm, mass_ref)))]
    own = pltpu.make_async_copy(sun_ref, recv.at[mine], loc_sem.at[8])
    for v in loads:
        v.start()
    pl.when(own_row)(lambda: own.start())

    def flag_copy(r, plane, d):
        return pltpu.make_async_remote_copy(
            src_ref=sun_ref, dst_ref=recv.at[r], send_sem=ssem.at[plane * 16 + d], recv_sem=rsem.at[r],
            device_id=device(plane, d), device_id_type=MESH)

    def table_copy():
        return pltpu.make_async_remote_copy(
            src_ref=recv, dst_ref=recv, send_sem=ssem.at[32], recv_sem=rsem.at[32],
            device_id={"span": q * 2 + 1 - zh}, device_id_type=MESH)

    def corner_copy():
        return pltpu.make_async_remote_copy(
            src_ref=sun_ref, dst_ref=recv.at[mine], send_sem=ssem.at[33], recv_sem=rsem.at[mine],
            device_id={"span": 1}, device_id_type=MESH)

    def start_copy(plane, d):
        flag_copy(mine, plane, d).start()

    def end_copy(plane, d):
        flag_copy(mine, plane, d).wait_send()

    def take_row(plane, d):
        flag_copy(plane * 16 + turn(d), plane, d).wait_recv()

    def send(when):
        @pl.when(when)
        def _():
            pl.semaphore_wait(barrier, expected)
            each(0, start_copy)
            pl.when(direct)(lambda: each(1, start_copy))
            pl.when(to_corner)(lambda: corner_copy().start())

    def take_rows(when):
        @pl.when(when)
        def _():
            own.wait()
            each(0, take_row)
            each(1, take_row)

    gives = first & jnp.logical_not(direct) & (q > 0)

    def hand_over():
        take_rows(gives)
        pl.when(gives)(lambda: table_copy().start())

    def finish_rows():
        take_rows(own_row & jnp.logical_not(gives))
        pl.when(jnp.logical_not(own_row))(lambda: table_copy().wait_recv())

    def end_copies():
        each(0, end_copy)
        pl.when(direct)(lambda: each(1, end_copy))
        pl.when(gives)(lambda: table_copy().wait_send())
        pl.when(to_corner)(lambda: corner_copy().wait_send())

    send(moment == 0)
    for v in loads:
        v.wait()

    for c in range(4):
        gas32[c] = gas_ref[:, :, cols(c)].reshape(GAS * L, LANES).astype(F32)
        bin32[c] = bin_ref[:, cols(c)].astype(F32)
    tab32[...] = jnp.zeros_like(tab32)
    for a in range(GAS):
        tab32[a * 64:a * 64 + 60, :G] = abs_ref[a].astype(F32)
    tab32[448:508, :G] = sca_ref[...].astype(F32) * 0.5
    lhs[...] = jnp.transpose(tab32[...])[:G].astype(BF16)
    kk = lax.broadcasted_iota(jnp.int32, (64, 256), 0).astype(F32).astype(BF16)

    def optics(l, tau_ref, h_ref, groups=(0, 1), after=None):
        for g in groups:
            def spread(ref, r):
                x = jnp.concatenate([wide_row(ref, 2 * g + k, r, 16) for k in range(2)], axis=1)
                if ref is bin32 and after is not None:
                    z = jnp.concatenate([after * 0.0] * 2, axis=0)
                    x = x + jnp.concatenate([z, z], axis=1)
                x = x.astype(BF16)
                return jnp.concatenate([x] * 4, axis=0)

            here = spread(bin32, l) == kk
            zero = jnp.zeros((64, 256), BF16)
            w = jnp.concatenate([jnp.where(here, spread(gas32, a * L + l), zero) for a in range(GAS)], axis=0)
            sel = jnp.where(here, jnp.ones_like(zero), zero)
            cs = slice(g * 256, g * 256 + 256)
            tau_ref[:, cs] = jnp.dot(lhs[:, :448], w, preferred_element_type=F32)
            h_ref[:, cs] = jnp.dot(lhs[:, 448:], sel, preferred_element_type=F32)

    optics(0, tau_a, h_a)
    mu = cos_ref[...].astype(F32).reshape(1, C)
    rate = -LOG2E / mu
    alb = alb_ref[...].astype(F32).reshape(1, C)
    for c in range(4):
        per_col[c, 0:1, :] = rate[:, cols(c)]
        per_col[c, 1:2, :] = alb[:, cols(c)]
    st_t[...] = jnp.ones_like(st_t)
    st_p[...] = jnp.zeros_like(st_p)
    st_q[...] = jnp.zeros_like(st_q)

    def layer(l, tau_ref, h_ref, tiles):
        seen = []
        for c in tiles:
            cs = cols(c)
            rate = wide_row(per_col, c, 0, 8)
            x = None
            for i in range(TILES):
                gs = rows(i)
                tau = tau_ref[gs, cs]
                h = h_ref[gs, cs]
                t0 = st_t[gs, cs]
                p0 = st_p[gs, cs]
                q0 = st_q[gs, cs]
                t1 = t0 * jnp.exp2(tau * rate)
                f = jnp.exp2(tau * FADE)
                r = h * (1.0 - f)
                t = f + r
                s = h * (t0 - t1)
                inv = pl.reciprocal(1.0 - r * p0, approx=False)
                ti = t * inv
                y = q0 + p0 * s
                st_t[gs, cs] = t1
                st_p[gs, cs] = r + t * (ti * p0)
                st_q[gs, cs] = s + ti * y
                ti_s[l, gs, cs] = ti
                v_s[l, gs, cs] = inv * (r * q0 + s)
                p_s[l, gs, cs] = p0
                x = t0 + q0 if x is None else x + (t0 + q0)
            acc[l, :, cs] = x
            seen.append(x)
        return seen

    def pair(k, carry):
        l = 2 * k
        send((k > 0) & (k == moment))
        n = jnp.minimum(l + 2, L - 1)
        x = layer(l, tau_a, h_a, (0, 1))
        optics(l + 1, tau_b, h_b, (0,))
        optics(l + 1, tau_b, h_b, (1,), x[0])
        y = layer(l, tau_a, h_a, (2, 3))
        x = layer(l + 1, tau_b, h_b, (0, 1))
        optics(n, tau_a, h_a, (0,), y[1])
        optics(n, tau_a, h_a, (1,), x[0])
        layer(l + 1, tau_b, h_b, (2, 3))
        return carry

    lax.fori_loop(0, L // 2, pair, 0)

    trow = lax.broadcasted_iota(jnp.int32, (8, C), 1)
    trow = (lax.rem(trow // 16, 2) * 16 + trow // 32).astype(F32).astype(BF16)
    order = order_ref[...].reshape(1, C)
    for c in range(4):
        hot = (lax.broadcasted_iota(jnp.int32, (LANES, C), 0) + c * LANES == order).astype(F32).astype(BF16)
        jcol[:, cols(c)] = lax.dot_general(trow, hot, (((1,), (1,)), ((), ())), preferred_element_type=F32)

    for half in range(2):
        where = [(rows(i), cols(c)) for c in (2 * half, 2 * half + 1) for i in range(TILES)]
        up0 = []
        sums = []
        for n, (gs, cs) in enumerate(where):
            al = wide_row(per_col, 2 * half + n // TILES, 1, 8)
            tt = st_t[gs, cs]
            pp = st_p[gs, cs]
            qq = st_q[gs, cs]
            u = al * (qq + tt) / (1.0 - al * pp)
            up0.append(u)
            sums.append(tt + (pp * u + qq) - u)
        for j in range(2):
            acc[L, :, cols(2 * half + j)] = sum(sums[j * TILES + 1:(j + 1) * TILES], sums[j * TILES])

        def up(k, u):
            for l in (L - 1 - 2 * k, L - 2 - 2 * k):
                u = [ti_s[l, gs, cs] * u[n] + v_s[l, gs, cs] for n, (gs, cs) in enumerate(where)]
                d = [p_s[l, gs, cs] * u[n] - u[n] for n, (gs, cs) in enumerate(where)]
                for j in range(2):
                    cs = cols(2 * half + j)
                    acc[l, :, cs] = acc[l, :, cs] + sum(d[j * TILES + 1:(j + 1) * TILES], d[j * TILES])
            return tuple(u)

        lax.fori_loop(0, L // 2, up, tuple(up0))
        if half == 0:
            hand_over()

    net = jnp.sum(acc[...], axis=1)
    heat[...] = (net[:L] - net[1:]) * (mu / mass_ref[...].astype(F32))
    finish_rows()
    flags = recv[...].reshape(32, 4)
    block = lax.broadcasted_iota(jnp.int32, (32, 4), 1) == me // 8
    flag = jnp.sum(jnp.where(block, flags, 0).astype(F32), axis=1, keepdims=True)
    j = lax.broadcasted_iota(jnp.int32, (32, C), 0).astype(F32)
    lit = jnp.sum(jnp.where(jnp.broadcast_to(jcol[0:1, :], (32, C)) == j, jnp.broadcast_to(flag, (32, C)), 0.0),
                  axis=0, keepdims=True)
    out_ref[...] = heat[...] * lit

    end_copies()


def local(gases, pressure_bin, layer_mass, cos_zenith, surface_albedo, column_order, sunlit, absorption, scattering):
    vm = pl.BlockSpec(memory_space=pltpu.VMEM)
    state = [pltpu.VMEM((G, C), F32)]
    return pl.pallas_call(
        body,
        out_shape=pltpu.VMEM((L, C), F32),
        in_specs=[pl.BlockSpec(memory_space=pl.ANY)] * 9,
        out_specs=vm,
        scratch_shapes=[
            pltpu.VMEM((GAS, L, C), BF16), pltpu.VMEM((L, C), jnp.int32), pltpu.VMEM((L, C), BF16),
            pltpu.VMEM((C,), BF16), pltpu.VMEM((C,), BF16), pltpu.VMEM((C,), jnp.int32),
            pltpu.VMEM((GAS, 60, G), BF16), pltpu.VMEM((60, G), BF16),
            pltpu.VMEM((4, GAS * L, LANES), F32), pltpu.VMEM((4, L, LANES), F32), pltpu.VMEM((C, LANES), F32),
            pltpu.VMEM((G, C), BF16)] + state * 7 + [pltpu.VMEM((L, G, C), F32)] * 3 + [
            pltpu.VMEM((L + 1, 8, C), F32), pltpu.VMEM((4, 8, LANES), F32),
            pltpu.VMEM((L, C), F32), pltpu.VMEM((32, 1, 4), jnp.int32), pltpu.VMEM((8, C), F32),
            pltpu.SemaphoreType.DMA((9,)), pltpu.SemaphoreType.DMA((34,)), pltpu.SemaphoreType.DMA((33,))],
        compiler_params=pltpu.CompilerParams(
            vmem_limit_bytes=60 * 1024 * 1024, collective_id=0, has_side_effects=True),
    )(gases, pressure_bin, layer_mass, cos_zenith, surface_albedo, column_order, sunlit.reshape(1, 4),
      jnp.transpose(absorption, (1, 2, 0)), jnp.transpose(scattering))


def solution(mesh):
    one = P(("band", "span"))
    two = P(None, ("band", "span"))
    return jax.shard_map(
        local, mesh=mesh, in_specs=(P(None, None, ("band", "span")), two, two, one, one, one, one, P(), P()),
        out_specs=two, check_vma=False)
```

```python
import jax
import jax.numpy as jnp
from jax import lax
from jax.experimental import pallas as pl
from jax.experimental.pallas import tpu as pltpu
from jax.sharding import PartitionSpec as P

MESH = pl.DeviceIdType.MESH
F32 = jnp.float32
BF16 = jnp.bfloat16
LOG2E = 1.4426950408889634
FADE = -1.66 * LOG2E
LANES = 128
GAS = 7
L = 32
G = 112
C = 512
TILES = G // 8


def wide_row(ref, c, row, n):
    return ref[c, pl.ds(row, n, stride=0), :]


def cols(c):
    return slice(c * LANES, (c + 1) * LANES)


def rows(i):
    return slice(i * 8, (i + 1) * 8)


def body(gas_hbm, bin_hbm, mass_hbm, cos_hbm, alb_hbm, order_hbm, sun_ref, abs_hbm, sca_hbm, out_ref,
         gas_ref, bin_ref, mass_ref, cos_ref, alb_ref, order_ref, abs_ref, sca_ref,
         gas32, bin32, tab32, lhs, tau_a, tau_b, h_a, h_b, st_t, st_p, st_q, ti_s, v_s, p_s, acc, per_col,
         heat, recv, jcol, loc_sem, ssem, rsem):
    me = lax.axis_index("span")
    q = me // 2
    zh = lax.rem(me, 2)
    x = q // 4
    y = lax.rem(q, 4)
    zl = lax.axis_index("band") // 2
    hops = jnp.minimum(x, 2) + jnp.minimum(y, 2)
    direct = zl >= 2
    first = zh == 0
    corner = (zh == 1) & (q == 0) & jnp.logical_not(direct)
    own_row = first | direct | corner
    to_corner = jnp.logical_not(direct | corner)
    mine = zh * 16 + q
    moment = jnp.where(direct, jnp.where(first, 35 - 3 * zl - 3 * hops, 9 + 3 * zl - 3 * hops),
                       jnp.where(first, 24 - 2 * hops, jnp.maximum(6 + 3 * zl - 3 * hops, 0))) // 2
    expected = jnp.where(direct, 31, jnp.where(first | corner, 16, 17))
    barrier = pltpu.get_barrier_semaphore()

    def turn(d):
        return lax.rem(q + d, 16)

    def device(plane, d):
        return {"span": turn(d) * 2 + plane}

    def each(plane, act):
        for d in range(16):
            if d:
                act(plane, d)
            else:
                pl.when(zh != plane)(lambda: act(plane, 0))

    def signal(plane, d):
        pl.semaphore_signal(barrier, inc=1, device_id=device(plane, d), device_id_type=MESH)

    loads = [pltpu.make_async_copy(src, dst, loc_sem.at[n]) for n, (src, dst) in enumerate((
        (abs_hbm, abs_ref), (sca_hbm, sca_ref), (gas_hbm, gas_ref), (bin_hbm, bin_ref), (cos_hbm, cos_ref),
        (alb_hbm, alb_ref), (order_hbm, order_ref), (mass_hbm, mass_ref)))]
    own = pltpu.make_async_copy(sun_ref, recv.at[mine], loc_sem.at[8])
    for v in loads:
        v.start()

    @pl.when(own_row)
    def _():
        each(1, signal)
        each(0, signal)
    pl.when(own_row)(lambda: own.start())

    def flag_copy(r, plane, d):
        return pltpu.make_async_remote_copy(
            src_ref=sun_ref, dst_ref=recv.at[r], send_sem=ssem.at[plane * 16 + d], recv_sem=rsem.at[r],
            device_id=device(plane, d), device_id_type=MESH)

    def table_copy():
        return pltpu.make_async_remote_copy(
            src_ref=recv, dst_ref=recv, send_sem=ssem.at[32], recv_sem=rsem.at[32],
            device_id={"span": q * 2 + 1 - zh}, device_id_type=MESH)

    def corner_copy():
        return pltpu.make_async_remote_copy(
            src_ref=sun_ref, dst_ref=recv.at[mine], send_sem=ssem.at[33], recv_sem=rsem.at[mine],
            device_id={"span": 1}, device_id_type=MESH)

    def start_copy(plane, d):
        flag_copy(mine, plane, d).start()

    def end_copy(plane, d):
        flag_copy(mine, plane, d).wait_send()

    def take_row(plane, d):
        flag_copy(plane * 16 + turn(d), plane, d).wait_recv()

    def send(when):
        @pl.when(when)
        def _():
            pl.semaphore_wait(barrier, expected)
            each(0, start_copy)
            pl.when(direct)(lambda: each(1, start_copy))
            pl.when(to_corner)(lambda: corner_copy().start())

    def take_rows(when):
        @pl.when(when)
        def _():
            own.wait()
            each(0, take_row)
            each(1, take_row)

    gives = first & jnp.logical_not(direct) & (q > 0)

    def hand_over():
        take_rows(gives)
        pl.when(gives)(lambda: table_copy().start())

    def finish_rows():
        take_rows(own_row & jnp.logical_not(gives))
        pl.when(jnp.logical_not(own_row))(lambda: table_copy().wait_recv())

    def end_copies():
        each(0, end_copy)
        pl.when(direct)(lambda: each(1, end_copy))
        pl.when(to_corner)(lambda: corner_copy().wait_send())

    send(moment == 0)
    loads[2].wait()
    loads[3].wait()
    for c in range(4):
        gas32[c] = gas_ref[:, :, cols(c)].reshape(GAS * L, LANES).astype(F32)
        bin32[c] = bin_ref[:, cols(c)].astype(F32)
    tab32[...] = jnp.zeros_like(tab32)
    loads[0].wait()
    loads[1].wait()
    for a in range(GAS):
        tab32[a * 64:a * 64 + 60, :G] = abs_ref[a].astype(F32)
    tab32[448:508, :G] = sca_ref[...].astype(F32) * 0.5
    lhs[...] = jnp.transpose(tab32[...])[:G].astype(BF16)
    kk = lax.broadcasted_iota(jnp.int32, (64, 256), 0).astype(F32).astype(BF16)

    def optics(l, tau_ref, h_ref, groups=(0, 1), after=None):
        for g in groups:
            def spread(ref, r):
                x = jnp.concatenate([wide_row(ref, 2 * g + k, r, 16) for k in range(2)], axis=1)
                if ref is bin32 and after is not None:
                    z = jnp.concatenate([after * 0.0] * 2, axis=0)
                    x = x + jnp.concatenate([z, z], axis=1)
                x = x.astype(BF16)
                return jnp.concatenate([x] * 4, axis=0)

            here = spread(bin32, l) == kk
            zero = jnp.zeros((64, 256), BF16)
            w = jnp.concatenate([jnp.where(here, spread(gas32, a * L + l), zero) for a in range(GAS)], axis=0)
            sel = jnp.where(here, jnp.ones_like(zero), zero)
            cs = slice(g * 256, g * 256 + 256)
            tau_ref[:, cs] = jnp.dot(lhs[:, :448], w, preferred_element_type=F32)
            h_ref[:, cs] = jnp.dot(lhs[:, 448:], sel, preferred_element_type=F32)

    optics(0, tau_a, h_a)
    for v in loads[4:]:
        v.wait()
    mu = cos_ref[...].astype(F32).reshape(1, C)
    rate = -LOG2E / mu
    alb = alb_ref[...].astype(F32).reshape(1, C)
    for c in range(4):
        per_col[c, 0:1, :] = rate[:, cols(c)]
        per_col[c, 1:2, :] = alb[:, cols(c)]
    st_t[...] = jnp.ones_like(st_t)
    st_p[...] = jnp.zeros_like(st_p)
    st_q[...] = jnp.zeros_like(st_q)

    def layer(l, tau_ref, h_ref, tiles):
        seen = []
        for c in tiles:
            cs = cols(c)
            rate = wide_row(per_col, c, 0, 8)
            x = None
            for i in range(TILES):
                gs = rows(i)
                tau = tau_ref[gs, cs]
                h = h_ref[gs, cs]
                t0 = st_t[gs, cs]
                p0 = st_p[gs, cs]
                q0 = st_q[gs, cs]
                t1 = t0 * jnp.exp2(tau * rate)
                f = jnp.exp2(tau * FADE)
                r = h * (1.0 - f)
                t = f + r
                s = h * (t0 - t1)
                inv = pl.reciprocal(1.0 - r * p0, approx=False)
                ti = t * inv
                y = q0 + p0 * s
                st_t[gs, cs] = t1
                st_p[gs, cs] = r + t * (ti * p0)
                st_q[gs, cs] = s + ti * y
                ti_s[l, gs, cs] = ti
                v_s[l, gs, cs] = inv * (r * q0 + s)
                p_s[l, gs, cs] = p0
                x = t0 + q0 if x is None else x + (t0 + q0)
            acc[l, :, cs] = x
            seen.append(x)
        return seen

    def pair(k, carry):
        l = 2 * k
        send((k > 0) & (k == moment))
        n = jnp.minimum(l + 2, L - 1)
        x = layer(l, tau_a, h_a, (0, 1))
        optics(l + 1, tau_b, h_b, (0,))
        optics(l + 1, tau_b, h_b, (1,), x[0])
        y = layer(l, tau_a, h_a, (2, 3))
        x = layer(l + 1, tau_b, h_b, (0, 1))
        optics(n, tau_a, h_a, (0,), y[1])
        optics(n, tau_a, h_a, (1,), x[0])
        layer(l + 1, tau_b, h_b, (2, 3))
        return carry

    lax.fori_loop(0, L // 2, pair, 0)

    trow = lax.broadcasted_iota(jnp.int32, (8, C), 1)
    trow = (lax.rem(trow // 16, 2) * 16 + trow // 32).astype(F32).astype(BF16)
    order = order_ref[...].reshape(1, C)
    for c in range(4):
        at = jnp.broadcast_to((order - c * LANES).astype(F32), (16, C)).astype(BF16)
        at = jnp.concatenate([at] * 8, axis=0) == lax.broadcasted_iota(jnp.int32, (LANES, C), 0).astype(F32).astype(BF16)
        hot = jnp.where(at, jnp.ones((LANES, C), BF16), jnp.zeros((LANES, C), BF16))
        jcol[:, cols(c)] = lax.dot_general(trow, hot, (((1,), (1,)), ((), ())), preferred_element_type=F32)

    for half in range(2):
        where = [(rows(i), cols(c)) for c in (2 * half, 2 * half + 1) for i in range(TILES)]
        up0 = []
        sums = []
        for n, (gs, cs) in enumerate(where):
            al = wide_row(per_col, 2 * half + n // TILES, 1, 8)
            tt = st_t[gs, cs]
            pp = st_p[gs, cs]
            qq = st_q[gs, cs]
            u = al * (qq + tt) / (1.0 - al * pp)
            up0.append(u)
            sums.append(tt + (pp * u + qq) - u)
        for j in range(2):
            acc[L, :, cols(2 * half + j)] = sum(sums[j * TILES + 1:(j + 1) * TILES], sums[j * TILES])

        def up(k, u):
            for l in [L - 1 - n - 4 * k for n in range(4)]:
                u = [ti_s[l, gs, cs] * u[n] + v_s[l, gs, cs] for n, (gs, cs) in enumerate(where)]
                d = [p_s[l, gs, cs] * u[n] - u[n] for n, (gs, cs) in enumerate(where)]
                for j in range(2):
                    cs = cols(2 * half + j)
                    acc[l, :, cs] = acc[l, :, cs] + sum(d[j * TILES + 1:(j + 1) * TILES], d[j * TILES])
            return tuple(u)

        lax.fori_loop(0, L // 4, up, tuple(up0))
        if half == 0:
            hand_over()

    net = jnp.sum(acc[...], axis=1)
    heat[...] = (net[:L] - net[1:]) * (mu / mass_ref[...].astype(F32))
    end_copies()
    finish_rows()
    flags = recv[...].reshape(32, 4)
    block = lax.broadcasted_iota(jnp.int32, (32, 4), 1) == me // 8
    flag = jnp.sum(jnp.where(block, flags, 0).astype(F32), axis=1, keepdims=True)
    j = lax.broadcasted_iota(jnp.int32, (32, C), 0).astype(F32)
    lit = jnp.sum(jnp.where(jnp.broadcast_to(jcol[0:1, :], (32, C)) == j, jnp.broadcast_to(flag, (32, C)), 0.0),
                  axis=0, keepdims=True)
    out_ref[...] = heat[...] * lit

    pl.when(gives)(lambda: table_copy().wait_send())


def local(gases, pressure_bin, layer_mass, cos_zenith, surface_albedo, column_order, sunlit, absorption, scattering):
    vm = pl.BlockSpec(memory_space=pltpu.VMEM)
    state = [pltpu.VMEM((G, C), F32)]
    return pl.pallas_call(
        body,
        out_shape=pltpu.VMEM((L, C), F32),
        in_specs=[pl.BlockSpec(memory_space=pl.ANY)] * 9,
        out_specs=vm,
        scratch_shapes=[
            pltpu.VMEM((GAS, L, C), BF16), pltpu.VMEM((L, C), jnp.int32), pltpu.VMEM((L, C), BF16),
            pltpu.VMEM((C,), BF16), pltpu.VMEM((C,), BF16), pltpu.VMEM((C,), jnp.int32),
            pltpu.VMEM((GAS, 60, G), BF16), pltpu.VMEM((60, G), BF16),
            pltpu.VMEM((4, GAS * L, LANES), F32), pltpu.VMEM((4, L, LANES), F32), pltpu.VMEM((C, LANES), F32),
            pltpu.VMEM((G, C), BF16)] + state * 7 + [pltpu.VMEM((L, G, C), F32)] * 3 + [
            pltpu.VMEM((L + 1, 8, C), F32), pltpu.VMEM((4, 8, LANES), F32),
            pltpu.VMEM((L, C), F32), pltpu.VMEM((32, 1, 4), jnp.int32), pltpu.VMEM((8, C), F32),
            pltpu.SemaphoreType.DMA((9,)), pltpu.SemaphoreType.DMA((34,)), pltpu.SemaphoreType.DMA((33,))],
        compiler_params=pltpu.CompilerParams(
            vmem_limit_bytes=60 * 1024 * 1024, collective_id=0, has_side_effects=True),
    )(gases, pressure_bin, layer_mass, cos_zenith, surface_albedo, column_order, sunlit.reshape(1, 4),
      jnp.transpose(absorption, (1, 2, 0)), jnp.transpose(scattering))


def solution(mesh):
    one = P(("band", "span"))
    two = P(None, ("band", "span"))
    return jax.shard_map(
        local, mesh=mesh, in_specs=(P(None, None, ("band", "span")), two, two, one, one, one, one, P(), P()),
        out_specs=two, check_vma=False)
```

```python
import jax
import jax.numpy as jnp
from jax import lax
from jax.experimental import pallas as pl
from jax.experimental.pallas import tpu as pltpu
from jax.sharding import PartitionSpec as P

MESH = pl.DeviceIdType.MESH
F32 = jnp.float32
BF16 = jnp.bfloat16
LOG2E = 1.4426950408889634
FADE = -1.66 * LOG2E
LANES = 128
GAS = 7
L = 32
G = 112
C = 512
TILES = G // 8


def wide_row(ref, c, row, n):
    return ref[c, pl.ds(row, n, stride=0), :]


def cols(c):
    return slice(c * LANES, (c + 1) * LANES)


def rows(i):
    return slice(i * 8, (i + 1) * 8)


def body(gas_hbm, bin_hbm, mass_hbm, cos_hbm, alb_hbm, order_hbm, sun_ref, abs_hbm, sca_hbm, out_ref,
         gas_ref, bin_ref, mass_ref, cos_ref, alb_ref, order_ref, abs_ref, sca_ref,
         gas32, bin32, tab32, lhs, tau_a, tau_b, h_a, h_b, st_t, st_p, st_q, ti_s, v_s, p_s, acc, per_col,
         heat, recv, jcol, loc_sem, ssem, rsem):
    me = lax.axis_index("span")
    q = me // 2
    zh = lax.rem(me, 2)
    x = q // 4
    y = lax.rem(q, 4)
    zl = lax.axis_index("band") // 2
    hops = jnp.minimum(x, 2) + jnp.minimum(y, 2)
    direct = zl >= 2
    first = zh == 0
    corner = (zh == 1) & (q == 0) & jnp.logical_not(direct)
    own_row = first | direct | corner
    to_corner = jnp.logical_not(direct | corner)
    mine = zh * 16 + q
    moment = jnp.where(direct, jnp.where(first, 31 - 2 * zl - 3 * hops, 6 + 3 * zl - 3 * hops),
                       jnp.where(first, 24 - 4 * zl - 2 * hops, jnp.maximum(6 + 3 * zl - 3 * hops, 0))) // 2
    expected = jnp.where(direct, 31, jnp.where(first | corner, 16, 17))
    barrier = pltpu.get_barrier_semaphore()

    def turn(d):
        return lax.rem(q + d, 16)

    def device(plane, d):
        return {"span": turn(d) * 2 + plane}

    def each(plane, act):
        for d in range(16):
            if d:
                act(plane, d)
            else:
                pl.when(zh != plane)(lambda: act(plane, 0))

    def signal(plane, d):
        pl.semaphore_signal(barrier, inc=1, device_id=device(plane, d), device_id_type=MESH)

    loads = [pltpu.make_async_copy(src, dst, loc_sem.at[n]) for n, (src, dst) in enumerate((
        (abs_hbm, abs_ref), (sca_hbm, sca_ref), (gas_hbm, gas_ref), (bin_hbm, bin_ref), (cos_hbm, cos_ref),
        (alb_hbm, alb_ref), (order_hbm, order_ref), (mass_hbm, mass_ref)))]
    own = pltpu.make_async_copy(sun_ref, recv.at[mine], loc_sem.at[8])
    for v in loads:
        v.start()

    @pl.when(own_row)
    def _():
        each(1, signal)
        each(0, signal)
    pl.when(own_row)(lambda: own.start())

    def flag_copy(r, plane, d):
        return pltpu.make_async_remote_copy(
            src_ref=sun_ref, dst_ref=recv.at[r], send_sem=ssem.at[plane * 16 + d], recv_sem=rsem.at[r],
            device_id=device(plane, d), device_id_type=MESH)

    def table_copy():
        return pltpu.make_async_remote_copy(
            src_ref=recv, dst_ref=recv, send_sem=ssem.at[32], recv_sem=rsem.at[32],
            device_id={"span": q * 2 + 1 - zh}, device_id_type=MESH)

    def corner_copy():
        return pltpu.make_async_remote_copy(
            src_ref=sun_ref, dst_ref=recv.at[mine], send_sem=ssem.at[33], recv_sem=rsem.at[mine],
            device_id={"span": 1}, device_id_type=MESH)

    def start_copy(plane, d):
        flag_copy(mine, plane, d).start()

    def end_copy(plane, d):
        flag_copy(mine, plane, d).wait_send()

    def take_row(plane, d):
        flag_copy(plane * 16 + turn(d), plane, d).wait_recv()

    def send(when):
        @pl.when(when)
        def _():
            pl.semaphore_wait(barrier, expected)
            each(0, start_copy)
            pl.when(direct)(lambda: each(1, start_copy))
            pl.when(to_corner)(lambda: corner_copy().start())

    def take_rows(when):
        @pl.when(when)
        def _():
            own.wait()
            each(0, take_row)
            each(1, take_row)

    gives = first & jnp.logical_not(direct) & (q > 0)

    def hand_over():
        take_rows(gives)
        pl.when(gives)(lambda: table_copy().start())

    def finish_rows():
        take_rows(own_row & jnp.logical_not(gives))
        pl.when(jnp.logical_not(own_row))(lambda: table_copy().wait_recv())

    def end_copies():
        each(0, end_copy)
        pl.when(direct)(lambda: each(1, end_copy))
        pl.when(to_corner)(lambda: corner_copy().wait_send())

    send(moment == 0)
    loads[2].wait()
    loads[3].wait()
    for c in range(4):
        gas32[c] = gas_ref[:, :, cols(c)].reshape(GAS * L, LANES).astype(F32)
        bin32[c] = bin_ref[:, cols(c)].astype(F32)
    tab32[...] = jnp.zeros_like(tab32)
    loads[0].wait()
    loads[1].wait()
    for a in range(GAS):
        tab32[a * 64:a * 64 + 60, :G] = abs_ref[a].astype(F32)
    tab32[448:508, :G] = sca_ref[...].astype(F32) * 0.5
    lhs[...] = jnp.transpose(tab32[...])[:G].astype(BF16)
    kk = lax.broadcasted_iota(jnp.int32, (64, 256), 0).astype(F32).astype(BF16)

    def optics(l, tau_ref, h_ref, groups=(0, 1), after=None):
        for g in groups:
            def spread(ref, r):
                x = jnp.concatenate([wide_row(ref, 2 * g + k, r, 16) for k in range(2)], axis=1)
                if ref is bin32 and after is not None:
                    z = jnp.concatenate([after * 0.0] * 2, axis=0)
                    x = x + jnp.concatenate([z, z], axis=1)
                x = x.astype(BF16)
                return jnp.concatenate([x] * 4, axis=0)

            here = spread(bin32, l) == kk
            zero = jnp.zeros((64, 256), BF16)
            w = jnp.concatenate([jnp.where(here, spread(gas32, a * L + l), zero) for a in range(GAS)], axis=0)
            sel = jnp.where(here, jnp.ones_like(zero), zero)
            cs = slice(g * 256, g * 256 + 256)
            tau_ref[:, cs] = jnp.dot(lhs[:, :448], w, preferred_element_type=F32)
            h_ref[:, cs] = jnp.dot(lhs[:, 448:], sel, preferred_element_type=F32)

    optics(0, tau_a, h_a)
    for v in loads[4:]:
        v.wait()
    mu = cos_ref[...].astype(F32).reshape(1, C)
    rate = -LOG2E / mu
    alb = alb_ref[...].astype(F32).reshape(1, C)
    for c in range(4):
        per_col[c, 0:1, :] = rate[:, cols(c)]
        per_col[c, 1:2, :] = alb[:, cols(c)]
    st_t[...] = jnp.ones_like(st_t)
    st_p[...] = jnp.zeros_like(st_p)
    st_q[...] = jnp.zeros_like(st_q)

    def layer(l, tau_ref, h_ref, tiles):
        seen = []
        for c in tiles:
            cs = cols(c)
            rate = wide_row(per_col, c, 0, 8)
            x = None
            for i in range(TILES):
                gs = rows(i)
                tau = tau_ref[gs, cs]
                h = h_ref[gs, cs]
                t0 = st_t[gs, cs]
                p0 = st_p[gs, cs]
                q0 = st_q[gs, cs]
                t1 = t0 * jnp.exp2(tau * rate)
                f = jnp.exp2(tau * FADE)
                r = h * (1.0 - f)
                t = f + r
                s = h * (t0 - t1)
                inv = pl.reciprocal(1.0 - r * p0, approx=False)
                ti = t * inv
                y = q0 + p0 * s
                st_t[gs, cs] = t1
                st_p[gs, cs] = r + t * (ti * p0)
                st_q[gs, cs] = s + ti * y
                ti_s[l, gs, cs] = ti
                v_s[l, gs, cs] = inv * (r * q0 + s)
                p_s[l, gs, cs] = p0
                x = t0 + q0 if x is None else x + (t0 + q0)
            acc[l, :, cs] = x
            seen.append(x)
        return seen

    def pair(k, carry):
        l = 2 * k
        send((k > 0) & (k == moment))
        n = jnp.minimum(l + 2, L - 1)
        x = layer(l, tau_a, h_a, (0, 1))
        optics(l + 1, tau_b, h_b, (0,))
        optics(l + 1, tau_b, h_b, (1,), x[0])
        y = layer(l, tau_a, h_a, (2, 3))
        x = layer(l + 1, tau_b, h_b, (0, 1))
        optics(n, tau_a, h_a, (0,), y[1])
        optics(n, tau_a, h_a, (1,), x[0])
        layer(l + 1, tau_b, h_b, (2, 3))
        return carry

    lax.fori_loop(0, L // 2, pair, 0)

    trow = lax.broadcasted_iota(jnp.int32, (8, C), 1)
    trow = (lax.rem(trow // 16, 2) * 16 + trow // 32).astype(F32).astype(BF16)
    order = order_ref[...].reshape(1, C)
    for c in range(4):
        at = jnp.broadcast_to((order - c * LANES).astype(F32), (16, C)).astype(BF16)
        at = jnp.concatenate([at] * 8, axis=0) == lax.broadcasted_iota(jnp.int32, (LANES, C), 0).astype(F32).astype(BF16)
        hot = jnp.where(at, jnp.ones((LANES, C), BF16), jnp.zeros((LANES, C), BF16))
        jcol[:, cols(c)] = lax.dot_general(trow, hot, (((1,), (1,)), ((), ())), preferred_element_type=F32)

    for half in range(2):
        where = [(rows(i), cols(c)) for c in (2 * half, 2 * half + 1) for i in range(TILES)]
        up0 = []
        sums = []
        for n, (gs, cs) in enumerate(where):
            al = wide_row(per_col, 2 * half + n // TILES, 1, 8)
            tt = st_t[gs, cs]
            pp = st_p[gs, cs]
            qq = st_q[gs, cs]
            u = al * (qq + tt) / (1.0 - al * pp)
            up0.append(u)
            sums.append(tt + (pp * u + qq) - u)
        for j in range(2):
            acc[L, :, cols(2 * half + j)] = sum(sums[j * TILES + 1:(j + 1) * TILES], sums[j * TILES])

        def up(k, u):
            for l in [L - 1 - n - 4 * k for n in range(4)]:
                u = [ti_s[l, gs, cs] * u[n] + v_s[l, gs, cs] for n, (gs, cs) in enumerate(where)]
                d = [p_s[l, gs, cs] * u[n] - u[n] for n, (gs, cs) in enumerate(where)]
                for j in range(2):
                    cs = cols(2 * half + j)
                    acc[l, :, cs] = acc[l, :, cs] + sum(d[j * TILES + 1:(j + 1) * TILES], d[j * TILES])
            return tuple(u)

        lax.fori_loop(0, L // 4, up, tuple(up0))
        if half == 0:
            hand_over()

    net = jnp.sum(acc[...], axis=1)
    heat[...] = (net[:L] - net[1:]) * (mu / mass_ref[...].astype(F32))
    end_copies()
    finish_rows()
    flags = recv[...].reshape(32, 4)
    block = lax.broadcasted_iota(jnp.int32, (32, 4), 1) == me // 8
    flag = jnp.sum(jnp.where(block, flags, 0).astype(F32), axis=1, keepdims=True)
    j = lax.broadcasted_iota(jnp.int32, (32, C), 0).astype(F32)
    lit = jnp.sum(jnp.where(jnp.broadcast_to(jcol[0:1, :], (32, C)) == j, jnp.broadcast_to(flag, (32, C)), 0.0),
                  axis=0, keepdims=True)
    out_ref[...] = heat[...] * lit

    pl.when(gives)(lambda: table_copy().wait_send())


def local(gases, pressure_bin, layer_mass, cos_zenith, surface_albedo, column_order, sunlit, absorption, scattering):
    vm = pl.BlockSpec(memory_space=pltpu.VMEM)
    state = [pltpu.VMEM((G, C), F32)]
    return pl.pallas_call(
        body,
        out_shape=pltpu.VMEM((L, C), F32),
        in_specs=[pl.BlockSpec(memory_space=pl.ANY)] * 9,
        out_specs=vm,
        scratch_shapes=[
            pltpu.VMEM((GAS, L, C), BF16), pltpu.VMEM((L, C), jnp.int32), pltpu.VMEM((L, C), BF16),
            pltpu.VMEM((C,), BF16), pltpu.VMEM((C,), BF16), pltpu.VMEM((C,), jnp.int32),
            pltpu.VMEM((GAS, 60, G), BF16), pltpu.VMEM((60, G), BF16),
            pltpu.VMEM((4, GAS * L, LANES), F32), pltpu.VMEM((4, L, LANES), F32), pltpu.VMEM((C, LANES), F32),
            pltpu.VMEM((G, C), BF16)] + state * 7 + [pltpu.VMEM((L, G, C), F32)] * 3 + [
            pltpu.VMEM((L + 1, 8, C), F32), pltpu.VMEM((4, 8, LANES), F32),
            pltpu.VMEM((L, C), F32), pltpu.VMEM((32, 1, 4), jnp.int32), pltpu.VMEM((8, C), F32),
            pltpu.SemaphoreType.DMA((9,)), pltpu.SemaphoreType.DMA((34,)), pltpu.SemaphoreType.DMA((33,))],
        compiler_params=pltpu.CompilerParams(
            vmem_limit_bytes=60 * 1024 * 1024, collective_id=0, has_side_effects=True),
    )(gases, pressure_bin, layer_mass, cos_zenith, surface_albedo, column_order, sunlit.reshape(1, 4),
      jnp.transpose(absorption, (1, 2, 0)), jnp.transpose(scattering))


def solution(mesh):
    one = P(("band", "span"))
    two = P(None, ("band", "span"))
    return jax.shard_map(
        local, mesh=mesh, in_specs=(P(None, None, ("band", "span")), two, two, one, one, one, one, P(), P()),
        out_specs=two, check_vma=False)
```

```python
import jax
import jax.numpy as jnp
from jax import lax
from jax.experimental import pallas as pl
from jax.experimental.pallas import tpu as pltpu
from jax.sharding import PartitionSpec as P

MESH = pl.DeviceIdType.MESH
F32 = jnp.float32
BF16 = jnp.bfloat16
LOG2E = 1.4426950408889634
FADE = -1.66 * LOG2E
LANES = 128
GAS = 7
L = 32
G = 112
C = 512
TILES = G // 8


def wide_row(ref, c, row, n):
    return ref[c, pl.ds(row, n, stride=0), :]


def cols(c):
    return slice(c * LANES, (c + 1) * LANES)


def rows(i):
    return slice(i * 8, (i + 1) * 8)


def body(gas_hbm, bin_hbm, mass_hbm, cos_hbm, alb_hbm, order_hbm, sun_ref, abs_hbm, sca_hbm, out_ref,
         gas_ref, bin_ref, mass_ref, cos_ref, alb_ref, order_ref, abs_ref, sca_ref,
         gas32, bin32, tab32, lhs, tau_a, tau_b, h_a, h_b, st_t, st_p, st_q, ti_s, v_s, p_s, acc, per_col,
         heat, recv, jcol, loc_sem, ssem, rsem):
    me = lax.axis_index("span")
    q = me // 2
    zh = lax.rem(me, 2)
    x = q // 4
    y = lax.rem(q, 4)
    zl = lax.axis_index("band") // 2
    hops = jnp.minimum(x, 2) + jnp.minimum(y, 2)
    direct = zl >= 2
    first = zh == 0
    corner = (zh == 1) & (q == 0) & jnp.logical_not(direct)
    own_row = first | direct | corner
    to_corner = jnp.logical_not(direct | corner)
    mine = zh * 16 + q
    moment = jnp.where(direct, jnp.where(first, 31 - 2 * zl - 3 * hops, 6 + 3 * zl - 3 * hops),
                       jnp.where(first, 24 - 4 * zl - 2 * hops, jnp.maximum(6 + 3 * zl - 3 * hops, 0))) // 2
    expected = jnp.where(direct, 31, jnp.where(first | corner, 16, 17))
    barrier = pltpu.get_barrier_semaphore()

    def turn(d):
        return lax.rem(q + d, 16)

    def device(plane, d):
        return {"span": turn(d) * 2 + plane}

    def each(plane, act):
        for d in range(16):
            if d:
                act(plane, d)
            else:
                pl.when(zh != plane)(lambda: act(plane, 0))

    def signal(plane, d):
        pl.semaphore_signal(barrier, inc=1, device_id=device(plane, d), device_id_type=MESH)

    loads = [pltpu.make_async_copy(src, dst, loc_sem.at[n]) for n, (src, dst) in enumerate((
        (abs_hbm, abs_ref), (sca_hbm, sca_ref), (gas_hbm, gas_ref), (bin_hbm, bin_ref), (cos_hbm, cos_ref),
        (alb_hbm, alb_ref), (order_hbm, order_ref), (mass_hbm, mass_ref)))]
    own = pltpu.make_async_copy(sun_ref, recv.at[mine], loc_sem.at[8])
    @pl.when(own_row)
    def _():
        each(1, signal)
        each(0, signal)

    for v in loads:
        v.start()

    pl.when(own_row)(lambda: own.start())

    def flag_copy(r, plane, d):
        return pltpu.make_async_remote_copy(
            src_ref=sun_ref, dst_ref=recv.at[r], send_sem=ssem.at[plane * 16 + d], recv_sem=rsem.at[r],
            device_id=device(plane, d), device_id_type=MESH)

    def table_copy():
        return pltpu.make_async_remote_copy(
            src_ref=recv, dst_ref=recv, send_sem=ssem.at[32], recv_sem=rsem.at[32],
            device_id={"span": q * 2 + 1 - zh}, device_id_type=MESH)

    def corner_copy():
        return pltpu.make_async_remote_copy(
            src_ref=sun_ref, dst_ref=recv.at[mine], send_sem=ssem.at[33], recv_sem=rsem.at[mine],
            device_id={"span": 1}, device_id_type=MESH)

    def start_copy(plane, d):
        flag_copy(mine, plane, d).start()

    def end_copy(plane, d):
        flag_copy(mine, plane, d).wait_send()

    def take_row(plane, d):
        flag_copy(plane * 16 + turn(d), plane, d).wait_recv()

    def send(when):
        @pl.when(when)
        def _():
            pl.semaphore_wait(barrier, expected)
            each(0, start_copy)
            pl.when(direct)(lambda: each(1, start_copy))
            pl.when(to_corner)(lambda: corner_copy().start())

    def take_rows(when):
        @pl.when(when)
        def _():
            own.wait()
            each(0, take_row)
            each(1, take_row)

    gives = first & jnp.logical_not(direct) & (q > 0)

    def hand_over():
        take_rows(gives)
        pl.when(gives)(lambda: table_copy().start())

    def finish_rows():
        take_rows(own_row & jnp.logical_not(gives))
        pl.when(jnp.logical_not(own_row))(lambda: table_copy().wait_recv())

    def end_copies():
        each(0, end_copy)
        pl.when(direct)(lambda: each(1, end_copy))
        pl.when(to_corner)(lambda: corner_copy().wait_send())

    send(moment == 0)
    loads[2].wait()
    loads[3].wait()
    for c in range(4):
        gas32[c] = gas_ref[:, :, cols(c)].reshape(GAS * L, LANES).astype(F32)
        bin32[c] = bin_ref[:, cols(c)].astype(F32)
    tab32[...] = jnp.zeros_like(tab32)
    loads[0].wait()
    loads[1].wait()
    for a in range(GAS):
        tab32[a * 64:a * 64 + 60, :G] = abs_ref[a].astype(F32)
    tab32[448:508, :G] = sca_ref[...].astype(F32) * 0.5
    lhs[...] = jnp.transpose(tab32[...])[:G].astype(BF16)
    kk = lax.broadcasted_iota(jnp.int32, (64, 256), 0).astype(F32).astype(BF16)

    def optics(l, tau_ref, h_ref, groups=(0, 1), after=None):
        for g in groups:
            def spread(ref, r):
                x = jnp.concatenate([wide_row(ref, 2 * g + k, r, 16) for k in range(2)], axis=1)
                if ref is bin32 and after is not None:
                    z = jnp.concatenate([after * 0.0] * 2, axis=0)
                    x = x + jnp.concatenate([z, z], axis=1)
                x = x.astype(BF16)
                return jnp.concatenate([x] * 4, axis=0)

            here = spread(bin32, l) == kk
            zero = jnp.zeros((64, 256), BF16)
            w = jnp.concatenate([jnp.where(here, spread(gas32, a * L + l), zero) for a in range(GAS)], axis=0)
            sel = jnp.where(here, jnp.ones_like(zero), zero)
            cs = slice(g * 256, g * 256 + 256)
            tau_ref[:, cs] = jnp.dot(lhs[:, :448], w, preferred_element_type=F32)
            h_ref[:, cs] = jnp.dot(lhs[:, 448:], sel, preferred_element_type=F32)

    optics(0, tau_a, h_a)
    for v in loads[4:]:
        v.wait()
    mu = cos_ref[...].astype(F32).reshape(1, C)
    rate = -LOG2E / mu
    alb = alb_ref[...].astype(F32).reshape(1, C)
    for c in range(4):
        per_col[c, 0:1, :] = rate[:, cols(c)]
        per_col[c, 1:2, :] = alb[:, cols(c)]
    st_t[...] = jnp.ones_like(st_t)
    st_p[...] = jnp.zeros_like(st_p)
    st_q[...] = jnp.zeros_like(st_q)

    def layer(l, tau_ref, h_ref, tiles):
        seen = []
        for c in tiles:
            cs = cols(c)
            rate = wide_row(per_col, c, 0, 8)
            x = None
            for i in range(TILES):
                gs = rows(i)
                tau = tau_ref[gs, cs]
                h = h_ref[gs, cs]
                t0 = st_t[gs, cs]
                p0 = st_p[gs, cs]
                q0 = st_q[gs, cs]
                t1 = t0 * jnp.exp2(tau * rate)
                f = jnp.exp2(tau * FADE)
                r = h * (1.0 - f)
                t = f + r
                s = h * (t0 - t1)
                inv = pl.reciprocal(1.0 - r * p0, approx=False)
                ti = t * inv
                y = q0 + p0 * s
                st_t[gs, cs] = t1
                st_p[gs, cs] = r + t * (ti * p0)
                st_q[gs, cs] = s + ti * y
                ti_s[l, gs, cs] = ti
                v_s[l, gs, cs] = inv * (r * q0 + s)
                p_s[l, gs, cs] = p0
                x = t0 + q0 if x is None else x + (t0 + q0)
            acc[l, :, cs] = x
            seen.append(x)
        return seen

    def pair(k, carry):
        l = 2 * k
        send((k > 0) & (k == moment))
        n = jnp.minimum(l + 2, L - 1)
        x = layer(l, tau_a, h_a, (0, 1))
        optics(l + 1, tau_b, h_b, (0,))
        optics(l + 1, tau_b, h_b, (1,), x[0])
        y = layer(l, tau_a, h_a, (2, 3))
        x = layer(l + 1, tau_b, h_b, (0, 1))
        optics(n, tau_a, h_a, (0,), y[1])
        optics(n, tau_a, h_a, (1,), x[0])
        layer(l + 1, tau_b, h_b, (2, 3))
        return carry

    lax.fori_loop(0, L // 2, pair, 0)

    trow = lax.broadcasted_iota(jnp.int32, (8, C), 1)
    trow = (lax.rem(trow // 16, 2) * 16 + trow // 32).astype(F32).astype(BF16)
    order = order_ref[...].reshape(1, C)
    for c in range(4):
        at = jnp.broadcast_to((order - c * LANES).astype(F32), (16, C)).astype(BF16)
        at = jnp.concatenate([at] * 8, axis=0) == lax.broadcasted_iota(jnp.int32, (LANES, C), 0).astype(F32).astype(BF16)
        hot = jnp.where(at, jnp.ones((LANES, C), BF16), jnp.zeros((LANES, C), BF16))
        jcol[:, cols(c)] = lax.dot_general(trow, hot, (((1,), (1,)), ((), ())), preferred_element_type=F32)

    for half in range(2):
        where = [(rows(i), cols(c)) for c in (2 * half, 2 * half + 1) for i in range(TILES)]
        up0 = []
        sums = []
        for n, (gs, cs) in enumerate(where):
            al = wide_row(per_col, 2 * half + n // TILES, 1, 8)
            tt = st_t[gs, cs]
            pp = st_p[gs, cs]
            qq = st_q[gs, cs]
            u = al * (qq + tt) / (1.0 - al * pp)
            up0.append(u)
            sums.append(tt + (pp * u + qq) - u)
        for j in range(2):
            acc[L, :, cols(2 * half + j)] = sum(sums[j * TILES + 1:(j + 1) * TILES], sums[j * TILES])

        def up(k, u):
            for l in [L - 1 - n - 4 * k for n in range(4)]:
                u = [ti_s[l, gs, cs] * u[n] + v_s[l, gs, cs] for n, (gs, cs) in enumerate(where)]
                d = [p_s[l, gs, cs] * u[n] - u[n] for n, (gs, cs) in enumerate(where)]
                for j in range(2):
                    cs = cols(2 * half + j)
                    acc[l, :, cs] = acc[l, :, cs] + sum(d[j * TILES + 1:(j + 1) * TILES], d[j * TILES])
            return tuple(u)

        lax.fori_loop(0, L // 4, up, tuple(up0))
        if half == 0:
            hand_over()

    net = jnp.sum(acc[...], axis=1)
    heat[...] = (net[:L] - net[1:]) * (mu / mass_ref[...].astype(F32))
    end_copies()
    finish_rows()
    flags = recv[...].reshape(32, 4)
    block = lax.broadcasted_iota(jnp.int32, (32, 4), 1) == me // 8
    flag = jnp.sum(jnp.where(block, flags, 0).astype(F32), axis=1, keepdims=True)
    j = lax.broadcasted_iota(jnp.int32, (32, C), 0).astype(F32)
    lit = jnp.sum(jnp.where(jnp.broadcast_to(jcol[0:1, :], (32, C)) == j, jnp.broadcast_to(flag, (32, C)), 0.0),
                  axis=0, keepdims=True)
    out_ref[...] = heat[...] * lit

    pl.when(gives)(lambda: table_copy().wait_send())


def local(gases, pressure_bin, layer_mass, cos_zenith, surface_albedo, column_order, sunlit, absorption, scattering):
    vm = pl.BlockSpec(memory_space=pltpu.VMEM)
    state = [pltpu.VMEM((G, C), F32)]
    return pl.pallas_call(
        body,
        out_shape=pltpu.VMEM((L, C), F32),
        in_specs=[pl.BlockSpec(memory_space=pl.ANY)] * 9,
        out_specs=vm,
        scratch_shapes=[
            pltpu.VMEM((GAS, L, C), BF16), pltpu.VMEM((L, C), jnp.int32), pltpu.VMEM((L, C), BF16),
            pltpu.VMEM((C,), BF16), pltpu.VMEM((C,), BF16), pltpu.VMEM((C,), jnp.int32),
            pltpu.VMEM((GAS, 60, G), BF16), pltpu.VMEM((60, G), BF16),
            pltpu.VMEM((4, GAS * L, LANES), F32), pltpu.VMEM((4, L, LANES), F32), pltpu.VMEM((C, LANES), F32),
            pltpu.VMEM((G, C), BF16)] + state * 7 + [pltpu.VMEM((L, G, C), F32)] * 3 + [
            pltpu.VMEM((L + 1, 8, C), F32), pltpu.VMEM((4, 8, LANES), F32),
            pltpu.VMEM((L, C), F32), pltpu.VMEM((32, 1, 4), jnp.int32), pltpu.VMEM((8, C), F32),
            pltpu.SemaphoreType.DMA((9,)), pltpu.SemaphoreType.DMA((34,)), pltpu.SemaphoreType.DMA((33,))],
        compiler_params=pltpu.CompilerParams(
            vmem_limit_bytes=60 * 1024 * 1024, collective_id=0, has_side_effects=True),
    )(gases, pressure_bin, layer_mass, cos_zenith, surface_albedo, column_order, sunlit.reshape(1, 4),
      jnp.transpose(absorption, (1, 2, 0)), jnp.transpose(scattering))


def solution(mesh):
    one = P(("band", "span"))
    two = P(None, ("band", "span"))
    return jax.shard_map(
        local, mesh=mesh, in_specs=(P(None, None, ("band", "span")), two, two, one, one, one, one, P(), P()),
        out_specs=two, check_vma=False)
```
